256 devices in a mesh: depth: 8 (over z_hi, x), space: 32 (over z_lo, y, core).
Axes of the slice: x: 4, y: 4, z: 8 (z_hi: 2, z_lo: 4; z = z_hi * 4 + z_lo), core: 2. Of those that a mesh axis runs over, the one named last changes fastest.
Arguments:
- c_points: float32 [8, 64, 128, 256], P('depth', None, 'space'), may hold values from -6 to 6
- adjoint_points: float32 [8, 64, 128, 256], P('depth', None, 'space'), may hold values from -6 to 6
- conv1_weight: bfloat16 [32, 64, 576], P('depth'), may hold values from -0.25 to 0.25
- conv2_weight: bfloat16 [32, 64, 576], P('depth'), may hold values from -0.25 to 0.25
- bias1: float32 [32, 64], P('depth'), may hold values from -3 to 3
Outputs:
- new_points: float32 [8, 64, 128, 256], P('depth', None, 'space')
- new_adjoints: float32 [8, 64, 128, 256], P('depth', None, 'space')
- grad_one: float32 [32, 64, 576], P('depth')
- grad_two: float32 [32, 64, 576], P('depth')
- grad_bias: float32 [32, 64], P('depth')
The draws below stay inside these ranges and needn't reach their ends.
All inputs are finite; a program needn't handle non-finite values.
Results may differ from the reference program's by a relative error of at most 0.006.
Values may be sent and summed in bfloat16 or wider, within the bound.
No kernel may reach another device: no remote copies, remote signals or barrier semaphores. Data moves between devices by JAX's collectives and lax.ppermute only.
A program may use at most 64 MiB of HBM per device.

```python
import math
import jax
import jax.numpy as jnp
from jax import lax

CHANNELS = 64
COLS = 256
LAYERS_DEV = 4
NROWS = 128
LAYERS = 32
N_DEPTH = 8


def block_levels(stream_key, shape, split, least, top_value):
    loudness, own = 1.0, jax.random.fold_in(stream_key, 6)
    for axis_at, blocks in split:
        draws = jnp.exp(jax.random.uniform(jax.random.fold_in(own, axis_at), (blocks,), jnp.float32, least / len(split), top_value / len(split)))
        loudness = loudness * jnp.repeat(draws, shape[axis_at] // blocks).reshape([-1 if axis == axis_at else 1 for axis in range(len(shape))])
    return loudness


def scatter_about(rng, extent, width, most, split=(), kind=jnp.bfloat16):
    values = width * jax.random.normal(rng, extent, jnp.float32)
    if split:
        values = values * block_levels(rng, extent, split, -0.22, 0.18)
    return jnp.clip(values, -most, most).astype(kind)


def setup_inputs(seed: int = 0) -> dict:
    splits = jax.random.split(jax.random.key(seed), 6)
    return {
        "c_points": scatter_about(splits[0], (N_DEPTH, CHANNELS, NROWS, COLS), 1.0, 6.0, ((0, 8), (2, 32)), jnp.float32),
        "adjoint_points": scatter_about(splits[1], (N_DEPTH, CHANNELS, NROWS, COLS), 1.0, 6.0, ((0, 8), (2, 32)), jnp.float32),
        "conv1_weight": scatter_about(splits[2], (LAYERS, CHANNELS, 9 * CHANNELS), (9 * CHANNELS) ** -0.5, 0.25, ((0, 8),)),
        "conv2_weight": scatter_about(splits[3], (LAYERS, CHANNELS, 9 * CHANNELS), (9 * CHANNELS) ** -0.5, 0.25, ((0, 8),)),
        "bias1": scatter_about(splits[4], (LAYERS, CHANNELS), 0.5, 3.0, ((0, 8),), jnp.float32),
    }


STEP = 0.25

def pad_both(field):
    return jnp.pad(field, ((0, 0), (1, 1), (1, 1)))

def tap_columns(padded, height, breadth):
    pieces = [padded[:, row_off:row_off + height, col_off:col_off + breadth] for row_off in range(3) for col_off in range(3)]
    return jnp.stack(pieces, 0).reshape(-1, height * breadth)

def flip_taps(padded, height, breadth):
    pieces = [padded[:, 2 - row_off:2 - row_off + height, 2 - col_off:2 - col_off + breadth] for row_off in range(3) for col_off in range(3)]
    return jnp.stack(pieces, 0).reshape(-1, height * breadth)

def transpose_weight(weight):
    chans = weight.shape[0]
    return weight.reshape(chans, 9, chans).transpose(2, 1, 0).reshape(chans, 9 * chans)

def outer_sum(left, right):
    return lax.dot_general(left, right, (((1,), (1,)), ((), ())), preferred_element_type=jnp.float32)

def reference(c_points, adjoint_points, conv1_weight, conv2_weight, bias1):
    height = NROWS
    breadth = COLS
    chans = CHANNELS
    scale = 1.0 / math.sqrt(NROWS * COLS)
    finals = []
    starts = []
    list_one = []
    list_two = []
    list_bias = []
    for group in range(N_DEPTH):
        current = c_points[group]
        saved = []
        for depth_pos in range(LAYERS_DEV):
            layer_num = group * LAYERS_DEV + depth_pos
            padded_in = pad_both(current.astype(jnp.bfloat16))
            pre = jnp.dot(conv1_weight[layer_num], tap_columns(padded_in, height, breadth), preferred_element_type=jnp.float32) + bias1[layer_num][:, None]
            hidden = jax.nn.softplus(pre).astype(jnp.bfloat16).reshape(chans, height, breadth)
            padded_hid = pad_both(hidden)
            branch = jnp.dot(conv2_weight[layer_num], tap_columns(padded_hid, height, breadth), preferred_element_type=jnp.float32)
            current = current + STEP * branch.reshape(chans, height, breadth)
            slope = 1.0 - jnp.exp(-hidden.astype(jnp.float32).reshape(chans, -1))
            saved.append((padded_in, padded_hid, slope))
        finals.append(current)
        adjoint = adjoint_points[group]
        grads_one = []
        grads_two = []
        grads_bias = []
        for depth_pos in reversed(range(LAYERS_DEV)):
            layer_num = group * LAYERS_DEV + depth_pos
            padded_in, padded_hid, slope = saved[depth_pos]
            scaled = (STEP * adjoint).astype(jnp.bfloat16)
            hidden_adj = jnp.dot(transpose_weight(conv2_weight[layer_num]), flip_taps(pad_both(scaled), height, breadth), preferred_element_type=jnp.float32)
            pre_adj = (hidden_adj * slope).astype(jnp.bfloat16)
            back = jnp.dot(transpose_weight(conv1_weight[layer_num]), flip_taps(pad_both(pre_adj.reshape(chans, height, breadth)), height, breadth), preferred_element_type=jnp.float32)
            adjoint = adjoint + back.reshape(chans, height, breadth)
            grads_two.append(outer_sum(scaled.reshape(chans, -1), tap_columns(padded_hid, height, breadth)) * scale)
            grads_one.append(outer_sum(pre_adj, tap_columns(padded_in, height, breadth)) * scale)
            grads_bias.append(lax.optimization_barrier(jnp.sum(pre_adj.astype(jnp.float32), axis=1)) * scale)
        starts.append(adjoint)
        list_one.extend(grads_one[::-1])
        list_two.extend(grads_two[::-1])
        list_bias.extend(grads_bias[::-1])
    new_points = jnp.stack([c_points[0]] + finals[:-1], 0)
    new_adjoints = jnp.stack(starts[1:] + [adjoint_points[N_DEPTH - 1]], 0)
    return (new_points, new_adjoints, jnp.stack(list_one, 0), jnp.stack(list_two, 0), jnp.stack(list_bias, 0))
```

```python
import functools
import math

import jax
import jax.numpy as jnp
from jax import lax
from jax.experimental import pallas as pl
from jax.experimental.pallas import tpu as pltpu
from jax.sharding import PartitionSpec as P


STEP = 0.25
F32 = jnp.float32
BF16 = jnp.bfloat16
VMEM = pltpu.VMEM


def lanes(j, breadth, rows=1):
    return slice(j * breadth, (j + rows) * breadth)


def put_stack(dst, j, row):
    chans, breadth = row.shape
    col = lax.broadcasted_iota(jnp.int32, row.shape, 1)
    left = jnp.where(col == 0, 0.0, pltpu.roll(row, 1, axis=1))
    right = jnp.where(col == breadth - 1, 0.0, pltpu.roll(row, breadth - 1, axis=1))
    dst[0:chans, lanes(j, breadth)] = left.astype(BF16)
    dst[chans : 2 * chans, lanes(j, breadth)] = row.astype(BF16)
    dst[2 * chans : 3 * chans, lanes(j, breadth)] = right.astype(BF16)


def conv(src, first, rows, weight, chans, breadth):
    one = two = None
    for j in range(0, rows + 2, 2):
        both = jnp.dot(weight, src[:, lanes(first + j, breadth, 2)], preferred_element_type=F32)
        for half in range(2):
            z = both[:, lanes(half, breadth)]
            k = j + half - 2
            if k >= 0:
                yield k, two + z[2 * chans :]
            two = one + z[chans : 2 * chans] if one is not None else None
            one = z[:chans]


def place():
    index = lax.axis_index("space")
    return index % 2 == 0, index > 0, index < lax.axis_size("space") - 1


def halo_rows(core, chip, even, breadth, row, depth=4, base=0):
    if row < 0:
        at = lanes(base + row + depth, breadth)
        return jnp.where(even, chip[:, at], core[:, at]).astype(F32)
    at = lanes(base + row - 4, breadth)
    return jnp.where(even, core[:, at], chip[:, at]).astype(F32)


def put_edges(near, far, base, even, breadth, rows):
    for k in range(2):
        below, above = rows[k].astype(BF16), rows[k + 2].astype(BF16)
        at = lanes(base + k, breadth)
        near[:, at] = jnp.where(even, above, below)
        far[:, at] = jnp.where(even, below, above)


def gate(value, row, low, high):
    if row < 0:
        return jnp.where(low, value, 0.0)
    if row >= 4:
        return jnp.where(high, value, 0.0)
    return value


def softplus(value):
    return jnp.maximum(value, 0.0) + jnp.log1p(jnp.exp(-jnp.abs(value)))


def entry_kernel(field, flat, flat16):
    _, _, height, breadth = field.shape
    for r in range(height):
        at = lanes(r, breadth)
        value = field[0, :, r, :]
        flat[:, at] = value
        flat16[:, at] = value.astype(BF16)


def prepare_kernel(q, w1, w2, bias, q4, b3, forward, columns):
    _, _, height, breadth = q.shape
    for r in range(height):
        at = lanes(r, breadth)
        value = q[0, :, r, :]
        q4[:, at] = value
        b3[:, at] = (STEP * value).astype(BF16)
    layers, chans, _ = w1.shape
    wide = 3 * chans
    for l in range(layers):
        for which, w in enumerate((w1, w2)):
            for dy in range(3):
                forward[l, which, dy * chans : (dy + 1) * chans, :] = w[l, :, dy * wide : (dy + 1) * wide]
    rows = jnp.concatenate([bias[...], jnp.zeros((8 - layers, chans), F32)], axis=0)
    columns[...] = jnp.concatenate([rows, jnp.zeros((8, 128 - chans), F32)], axis=1).T


def turn_kernel(w1, w2, backward):
    layers, chans, _ = w1.shape
    for l in range(layers):
        for which, w in enumerate((w1, w2)):
            turned = w[l].astype(F32).T
            for e in range(3):
                blocks = [turned[(8 - 3 * e - s) * chans : (9 - 3 * e - s) * chans] for s in range(3)]
                backward[l, which, e * chans : (e + 1) * chans, :] = jnp.concatenate(blocks, axis=1).astype(BF16)


def forward_kernel(pos, state, core, chip, weights, bias, b, out, near, far, out16, xa, aa, xb, ab, xs, mid):
    chans, breadth = state.shape[0], state.shape[1] // 4
    even, low, high = place()

    def start(row):
        if 0 <= row < 4:
            return state[:, lanes(row, breadth)]
        return halo_rows(core, chip, even, breadth, row)

    for row in range(-4, 8):
        put_stack(xs, row + 4, start(row))
    xa[...] = xs[:, lanes(3, breadth, 6)]
    offset = bias[0:chans, pos : pos + 1]
    for k, value in conv(xs, 0, 10, weights[pos, 0], chans, breadth):
        put_stack(aa, k, gate(softplus(value + offset), k - 3, low, high))
    for k, value in conv(aa, 0, 8, weights[pos, 1], chans, breadth):
        row = k - 2
        value = gate(start(row) + STEP * value, row, low, high)
        put_stack(xs, k, value)
        mid[:, lanes(k, breadth)] = value
    xb[...] = xs[:, lanes(1, breadth, 6)]
    offset = bias[0:chans, pos + 1 : pos + 2]
    for k, value in conv(xs, 0, 6, weights[pos + 1, 0], chans, breadth):
        put_stack(ab, k, gate(softplus(value + offset), k - 1, low, high))
    for k, value in conv(ab, 0, 4, weights[pos + 1, 1], chans, breadth):
        value = mid[:, lanes(k + 2, breadth)] + STEP * value
        if out is None:
            out16[:, lanes(k, breadth)] = value.astype(BF16)
        else:
            out[:, lanes(k, breadth)] = value
            near[:, lanes(k, breadth)] = value.astype(BF16)
            far[:, lanes(k, breadth)] = value.astype(BF16)
    if out is not None:
        put_edges(near, far, 4, even, breadth, [b[:, lanes(k, breadth)] for k in range(4)])


def slope(stack, j, chans, breadth):
    return 1.0 - jnp.exp(-stack[chans : 2 * chans, lanes(j, breadth)].astype(F32))


def single_kernel(pos, skip, base, adjoint, core, chip, hidden, weights, final, outs, e16, bs, es):
    chans, breadth = adjoint.shape[0], adjoint.shape[1] // 4
    even, low, high = place()
    for row in range(-2, 6):
        if 0 <= row < 4:
            value = STEP * adjoint[:, lanes(row, breadth)]
            if final is not None:
                outs[2][:, lanes(row, breadth)] = value.astype(BF16)
        else:
            value = halo_rows(core, chip, even, breadth, row, 2, base)
        put_stack(bs, row + 2, value)
    for k, value in conv(bs, 0, 6, weights[pos, 1], chans, breadth):
        row = k - 1
        value = gate(value * slope(hidden, k + skip, chans, breadth), row, low, high)
        if 0 <= row < 4:
            e16[:, lanes(row, breadth)] = value.astype(BF16)
        put_stack(es, k, value)
    for k, value in conv(es, 0, 4, weights[pos, 0], chans, breadth):
        at = lanes(k, breadth)
        value = adjoint[:, at] + value
        if final is None:
            outs[0][:, at] = value
            outs[1][:, at] = (STEP * value).astype(BF16)
        else:
            value = value.astype(BF16)
            outs[0][:, at] = jnp.where(even_group(), final[:, at], value)
            outs[1][:, at] = jnp.where(even_group(), value, final[:, at])


def even_group():
    return lax.axis_index("depth") % 2 == 0


def double_kernel(pos, adjoint, core, chip, ha, hb, weights, out, near, far, ba16, ea16, bb16, eb16, bs, es, mid):
    chans, breadth = adjoint.shape[0], adjoint.shape[1] // 4
    even, low, high = place()
    for row in range(-4, 8):
        if 0 <= row < 4:
            value = STEP * adjoint[:, lanes(row, breadth)]
            ba16[:, lanes(row, breadth)] = value.astype(BF16)
        else:
            value = halo_rows(core, chip, even, breadth, row)
        put_stack(bs, row + 4, value)
    for k, value in conv(bs, 0, 10, weights[pos, 1], chans, breadth):
        row = k - 3
        value = gate(value * slope(ha, k, chans, breadth), row, low, high)
        if 0 <= row < 4:
            ea16[:, lanes(row, breadth)] = value.astype(BF16)
        put_stack(es, k, value)
    for k, value in conv(es, 0, 8, weights[pos, 0], chans, breadth):
        row = k - 2
        if 0 <= row < 4:
            value = adjoint[:, lanes(row, breadth)] + value
        else:
            value = 4.0 * halo_rows(core, chip, even, breadth, row) + value
        value = gate(value, row, low, high)
        mid[:, lanes(k, breadth)] = value
        value = STEP * value
        if 0 <= row < 4:
            bb16[:, lanes(row, breadth)] = value.astype(BF16)
        put_stack(bs, k, value)
    for k, value in conv(bs, 0, 6, weights[pos - 1, 1], chans, breadth):
        row = k - 1
        value = gate(value * slope(hb, k, chans, breadth), row, low, high)
        if 0 <= row < 4:
            eb16[:, lanes(row, breadth)] = value.astype(BF16)
        put_stack(es, k, value)
    rows = []
    for k, value in conv(es, 0, 4, weights[pos - 1, 0], chans, breadth):
        value = mid[:, lanes(k + 2, breadth)] + value
        out[:, lanes(k, breadth)] = value
        rows.append(STEP * value)
    put_edges(near, far, 0, even, breadth, rows)


def outer(left, right):
    return lax.dot_general(left, right, (((1,), (1,)), ((), ())), preferred_element_type=F32)


def grad_kernel(skip, b, hidden, e, inputs, pay, bd, ed):
    chans, breadth = b.shape[0], b.shape[1] // 4
    for src, dst in ((b, bd), (e, ed)):
        dst[...] = jnp.zeros_like(dst)
        for dy in range(3):
            dst[dy * chans : (dy + 1) * chans, lanes(dy, breadth, 4)] = src[...]
    two = outer(bd[...], hidden[:, lanes(skip, breadth, 6)])
    one = outer(ed[...], inputs[...])
    both = jnp.concatenate([two, one], axis=1)
    for c in range(8):
        for t in range(3):
            pay[c, 24 * t : 24 * t + 24, :] = both[24 * c : 24 * c + 24, 128 * t : 128 * t + 128]
        pay[c, 72:80, :] = jnp.zeros((8, 128), F32)
    ones = jnp.ones((8, e.shape[1]), BF16)
    pay[0, 72:73, 0:chans] = outer(ones, e[...])[0:1]


def packed(total):
    body = total[..., 0:72, :].astype(BF16)
    tail = total[..., 72:80, :]
    bias = tail[..., 0:1, :] + tail[..., 1:2, :]
    head = bias.astype(BF16).astype(F32)
    row = lax.broadcasted_iota(jnp.int32, tail.shape, tail.ndim - 2)
    tail = jnp.where(row == 0, head, jnp.where(row == 1, bias - head, 0.0))
    return body, tail.astype(BF16)


def where_am_i():
    index = lax.axis_index("space")
    return index % 2, (index // 2) % 4, index // 8


def split_kernel(g0, g1, g2, g3, send, keep):
    core, _, _ = where_am_i()
    for k in range(8):
        for at, low, high in ((k, g0, g2), (k + 8, g1, g3)):
            a, b = low[k], high[k]
            keep[at] = jnp.where(core == 0, a, b)
            body, tail = packed(jnp.where(core == 0, b, a))
            send[at, 0:72] = body
            send[at, 72:80] = tail


def spread_kernel(axis, keep_in, *refs):
    *parts, keep, send1, send2, send3 = refs
    mine = where_am_i()[axis]
    count = keep.shape[0]
    for k, dst in enumerate((keep, send1, send2, send3)):
        other = mine ^ k
        for n in range(count):
            at = other * count + n
            total = keep_in[at]
            for part in parts:
                total = total + part[at].astype(F32)
            if k == 0:
                dst[n] = total
            else:
                body, tail = packed(total)
                dst[n, 0:72] = body
                dst[n, 72:80] = tail


def total_kernel(keep, part1, part2, part3, out):
    total = keep[0] + part1[0].astype(F32) + part2[0].astype(F32) + part3[0].astype(F32)
    body, tail = packed(total)
    out[0, 0:72] = body
    out[0, 72:80] = tail


def join_kernel(axis, own, part1, part2, part3, out):
    mine = where_am_i()[axis]
    count = own.shape[0]
    for k, src in enumerate((own, part1, part2, part3)):
        for n in range(count):
            out[(mine ^ k) * count + n] = src[n]


def points_kernel(c, q, pair, far, points, adjoints):
    _, _, height, breadth = c.shape
    group = lax.axis_index("depth")
    first, last = group == 0, group == lax.axis_size("depth") - 1
    for r in range(height):
        at = lanes(r, breadth)
        a, b = pair[:, at].astype(F32), far[:, at].astype(F32)
        points[0, :, r, :] = jnp.where(first, c[0, :, r, :], jnp.where(even_group(), b, a))
        adjoints[0, :, r, :] = jnp.where(last, q[0, :, r, :], jnp.where(even_group(), a, b))


def exit_kernel(scale, own, part, one, two, bias):
    chans = one.shape[1]
    core, _, _ = where_am_i()
    wide = 3 * chans
    for l in range(one.shape[0]):
        base = 8 * (l % 2)

        def piece(k, rows, width=128):
            a, b = own[base + k, rows, 0:width].astype(F32), part[base + k, rows, 0:width].astype(F32)
            return jnp.where(core == l // 2, a, b)

        cols = [
            jnp.concatenate([piece(k, slice(24 * t, 24 * t + 24)) for k in range(8)], axis=0)
            for t in range(3)
        ]
        full = jnp.concatenate(cols, axis=1) * scale
        for dy in range(3):
            rows = full[dy * chans : (dy + 1) * chans]
            two[l, :, dy * wide : (dy + 1) * wide] = rows[:, :wide]
            one[l, :, dy * wide : (dy + 1) * wide] = rows[:, wide:]
        low = piece(0, slice(72, 74), chans)
        bias[l : l + 1, :] = (low[0:1] + low[1:2]) * scale


def call(kernel, outs, args, scratch=(), flops=0):
    size = sum(math.prod(a.shape) * a.dtype.itemsize for a in (*args, *outs))
    return pl.pallas_call(
        kernel,
        out_shape=outs,
        in_specs=[pl.BlockSpec(memory_space=VMEM) for _ in args],
        out_specs=[pl.BlockSpec(memory_space=VMEM) for _ in outs],
        scratch_shapes=list(scratch),
        cost_estimate=pl.CostEstimate(flops=flops, bytes_accessed=size, transcendentals=0),
        compiler_params=pltpu.CompilerParams(vmem_limit_bytes=40 << 20),
    )(*args)


def swaps(near, far):
    count = lax.axis_size("space")
    core = [(i, i ^ 1) for i in range(count)]
    chip = [(i, i + 1 if i % 2 else i - 1) for i in range(1, count - 1)]
    far = lax.ppermute(far, "space", chip)
    near = lax.ppermute(near, "space", core)
    return near, far


def partner(value, mask):
    return lax.ppermute(value, "space", [(i, i ^ mask) for i in range(lax.axis_size("space"))])


def pairs_of_groups(block, first):
    count = lax.axis_size("depth")
    pairs = [(i, i + 1) for i in range(first, count - 1, 2)]
    return lax.ppermute(block, "depth", pairs + [(b, a) for a, b in pairs])


def body(c_points, adjoint_points, conv1_weight, conv2_weight, bias1):
    _, chans, height, breadth = c_points.shape
    layers = conv1_weight.shape[0]
    tiles = lax.axis_size("space")
    scale = 1.0 / math.sqrt(height * tiles * breadth)
    pix = height * breadth
    wide = 3 * chans
    S = jax.ShapeDtypeStruct
    tile32, tile16 = S((chans, pix), F32), S((chans, pix), BF16)
    rows16 = lambda rows: S((chans, rows * breadth), BF16)
    stack = lambda rows: S((wide, rows * breadth), BF16)
    row_flops = 2 * wide * wide * breadth

    s0, s0h = call(entry_kernel, [tile32, tile16], [c_points])
    near1, far1 = swaps(s0h, s0h)
    mats = S((layers, 2, wide, wide), BF16)
    q4, b3, fw, bias = call(
        prepare_kernel, [tile32, tile16, mats, S((128, 8), F32)], [adjoint_points, conv1_weight, conv2_weight, bias1]
    )
    bw = call(turn_kernel, [mats], [conv1_weight, conv2_weight])[0]

    def forward(pos, state, core, chip, last):
        saved = [stack(6), stack(10), stack(6), stack(6)]
        if last:
            outs = [tile16, *saved]
            kernel = lambda st, co, ch, w, b, *rest: forward_kernel(pos, st, co, ch, w, b, None, None, None, None, *rest)
            args = [state, core, chip, fw, bias]
        else:
            outs = [tile32, rows16(6), rows16(6), *saved]

            def kernel(st, co, ch, w, b, edge, out, near, far, *rest):
                forward_kernel(pos, st, co, ch, w, b, edge, out, near, far, None, *rest)

            args = [state, core, chip, fw, bias, b3]
        return call(
            kernel,
            outs,
            args,
            [VMEM((wide, 12 * breadth), BF16), VMEM((chans, 8 * breadth), F32)],
            flops=36 * row_flops,
        )

    s2, near2, far2, x0, a0, x1, a1 = forward(0, s0, near1, far1, False)
    near2, far2 = swaps(near2, far2)
    f16, x2, a2, x3, a3 = forward(2, s2, near2, far2, True)

    def single(pos, skip, base, adjoint, core, chip, hidden, final):
        outs = [tile32, tile16] if final is None else [tile16] * 3
        args = [adjoint, core, chip, hidden, bw]

        def kernel(*refs):
            given, refs = refs[: len(args)], refs[len(args) :]
            held = None if final is None else given[5]
            results, rest = refs[: len(outs)], refs[len(outs) :]
            single_kernel(pos, skip, base, *given[:5], held, results, *rest)

        if final is not None:
            args.append(final)
        return call(
            kernel,
            [*outs, tile16],
            args,
            [VMEM((wide, 8 * breadth), BF16), VMEM((wide, 6 * breadth), BF16)],
            flops=14 * row_flops,
        )

    def grads(skip, b, hidden, e, inputs):
        return call(
            functools.partial(grad_kernel, skip),
            [S((8, 80, 128), F32)],
            [b, hidden, e, inputs],
            [VMEM((wide, 6 * breadth), BF16)] * 2,
            flops=12 * row_flops,
        )[0]

    q3, b2h, e3 = single(3, 0, 4, q4, near2, far2, a3, None)
    near3, far3 = swaps(b2h, b2h)
    g3 = grads(0, b3, a3, e3, x3)
    q1, near4, far4, b2, e2, b1, e1 = call(
        functools.partial(double_kernel, 2),
        [tile32, rows16(2), rows16(2), tile16, tile16, tile16, tile16],
        [q3, near3, far3, a2, a1, bw],
        [VMEM((wide, 12 * breadth), BF16), VMEM((wide, 10 * breadth), BF16), VMEM((chans, 8 * breadth), F32)],
        flops=36 * row_flops,
    )
    near4, far4, g3 = lax.optimization_barrier((near4, far4, g3))
    near4, far4 = swaps(near4, far4)
    g2 = grads(2, b2, a2, e2, x2)
    g1 = grads(0, b1, a1, e1, x1)
    pair, far, b0, e0 = single(0, 2, 0, q1, near4, far4, a0, f16)
    g0 = grads(2, b0, a0, e0, x0)

    def chunks(n, kind):
        return S((n, 80, 128), kind)

    send, keep = call(split_kernel, [chunks(16, BF16), chunks(16, F32)], [g0, g1, g2, g3])
    parts = [partner(send, 1)]
    for axis, step, count in ((1, 2, 4), (2, 8, 1)):
        keep, *sends = call(
            functools.partial(spread_kernel, axis), [chunks(count, F32)] + [chunks(count, BF16)] * 3, [keep, *parts]
        )
        parts = [partner(value, step * (k + 1)) for k, value in enumerate(sends)]
    far = pairs_of_groups(far, 1)
    pair = pairs_of_groups(pair, 0)
    mine = call(total_kernel, [chunks(1, BF16)], [keep, *parts])[0]
    parts = [partner(mine, 8 * (k + 1)) for k in range(3)]
    mine = call(functools.partial(join_kernel, 2), [chunks(4, BF16)], [mine, *parts])[0]
    mine, pair, far = lax.optimization_barrier((mine, pair, far))
    parts = [partner(mine, 2 * (k + 1)) for k in range(3)]
    points, adjoints = call(
        points_kernel, [S(c_points.shape, F32), S(c_points.shape, F32)], [c_points, adjoint_points, pair, far]
    )
    mine = call(functools.partial(join_kernel, 1), [chunks(16, BF16)], [mine, *parts])[0]
    mine, points, adjoints = lax.optimization_barrier((mine, points, adjoints))
    grad = S(conv1_weight.shape, F32)
    one, two, vec = call(
        functools.partial(exit_kernel, scale), [grad, grad, S(bias1.shape, F32)], [mine, partner(mine, 1)]
    )
    return points, adjoints, one, two, vec


def solution(mesh):
    in_specs = (
        P("depth", None, "space", None),
        P("depth", None, "space", None),
        P("depth", None, None),
        P("depth", None, None),
        P("depth", None),
    )
    out_specs = in_specs[:2] + (P("depth", None, None), P("depth", None, None), P("depth", None))

    def run(*args):
        return tuple(body(*args))

    return jax.shard_map(run, mesh=mesh, in_specs=in_specs, out_specs=out_specs, check_vma=False)
```

```python
import functools
import math

import jax
import jax.numpy as jnp
from jax import lax
from jax.experimental import pallas as pl
from jax.experimental.pallas import tpu as pltpu
from jax.sharding import PartitionSpec as P


STEP = 0.25
F32 = jnp.float32
BF16 = jnp.bfloat16
VMEM = pltpu.VMEM


def lanes(j, breadth, rows=1):
    return slice(j * breadth, (j + rows) * breadth)


def put_stack(dst, j, row):
    chans, breadth = row.shape
    col = lax.broadcasted_iota(jnp.int32, row.shape, 1)
    left = jnp.where(col == 0, 0.0, pltpu.roll(row, 1, axis=1))
    right = jnp.where(col == breadth - 1, 0.0, pltpu.roll(row, breadth - 1, axis=1))
    dst[0:chans, lanes(j, breadth)] = left.astype(BF16)
    dst[chans : 2 * chans, lanes(j, breadth)] = row.astype(BF16)
    dst[2 * chans : 3 * chans, lanes(j, breadth)] = right.astype(BF16)


def conv(src, first, rows, weight, chans, breadth):
    one = two = None
    for j in range(0, rows + 2, 2):
        both = jnp.dot(weight, src[:, lanes(first + j, breadth, 2)], preferred_element_type=F32)
        for half in range(2):
            z = both[:, lanes(half, breadth)]
            k = j + half - 2
            if k >= 0:
                yield k, two + z[2 * chans :]
            two = one + z[chans : 2 * chans] if one is not None else None
            one = z[:chans]


def place():
    index = lax.axis_index("space")
    return index % 2 == 0, index > 0, index < lax.axis_size("space") - 1


def halo_rows(core, chip, even, breadth, row, depth=4, base=0):
    if row < 0:
        at = lanes(base + row + depth, breadth)
        return jnp.where(even, chip[:, at], core[:, at]).astype(F32)
    at = lanes(base + row - 4, breadth)
    return jnp.where(even, core[:, at], chip[:, at]).astype(F32)


def put_edges(near, far, base, even, breadth, rows):
    for k in range(2):
        below, above = rows[k].astype(BF16), rows[k + 2].astype(BF16)
        at = lanes(base + k, breadth)
        near[:, at] = jnp.where(even, above, below)
        far[:, at] = jnp.where(even, below, above)


def gate(value, row, low, high):
    if row < 0:
        return jnp.where(low, value, 0.0)
    if row >= 4:
        return jnp.where(high, value, 0.0)
    return value


def softplus(value):
    return jnp.maximum(value, 0.0) + jnp.log1p(jnp.exp(-jnp.abs(value)))


def entry_kernel(field, flat, flat16):
    _, _, height, breadth = field.shape
    for r in range(height):
        at = lanes(r, breadth)
        value = field[0, :, r, :]
        flat[:, at] = value
        flat16[:, at] = value.astype(BF16)


def prepare_kernel(q, w1, w2, bias, q4, b3, forward, columns):
    _, _, height, breadth = q.shape
    for r in range(height):
        at = lanes(r, breadth)
        value = q[0, :, r, :]
        q4[:, at] = value
        b3[:, at] = (STEP * value).astype(BF16)
    layers, chans, _ = w1.shape
    wide = 3 * chans
    for l in range(layers):
        for which, w in enumerate((w1, w2)):
            for dy in range(3):
                forward[l, which, dy * chans : (dy + 1) * chans, :] = w[l, :, dy * wide : (dy + 1) * wide]
    rows = jnp.concatenate([bias[...], jnp.zeros((8 - layers, chans), F32)], axis=0)
    columns[...] = jnp.concatenate([rows, jnp.zeros((8, 128 - chans), F32)], axis=1).T


def turn_kernel(w1, w2, backward):
    layers, chans, _ = w1.shape
    for l in range(layers):
        for which, w in enumerate((w1, w2)):
            turned = w[l].astype(F32).T
            for e in range(3):
                blocks = [turned[(8 - 3 * e - s) * chans : (9 - 3 * e - s) * chans] for s in range(3)]
                backward[l, which, e * chans : (e + 1) * chans, :] = jnp.concatenate(blocks, axis=1).astype(BF16)


def forward_kernel(pos, state, core, chip, weights, bias, b, out, near, far, out16, xa, aa, xb, ab, xs, mid):
    chans, breadth = state.shape[0], state.shape[1] // 4
    even, low, high = place()

    def start(row):
        if 0 <= row < 4:
            return state[:, lanes(row, breadth)]
        return halo_rows(core, chip, even, breadth, row)

    for row in range(-4, 8):
        put_stack(xs, row + 4, start(row))
    xa[...] = xs[:, lanes(3, breadth, 6)]
    offset = bias[0:chans, pos : pos + 1]
    for k, value in conv(xs, 0, 10, weights[pos, 0], chans, breadth):
        put_stack(aa, k, gate(softplus(value + offset), k - 3, low, high))
    for k, value in conv(aa, 0, 8, weights[pos, 1], chans, breadth):
        row = k - 2
        value = gate(start(row) + STEP * value, row, low, high)
        put_stack(xs, k, value)
        mid[:, lanes(k, breadth)] = value
    xb[...] = xs[:, lanes(1, breadth, 6)]
    offset = bias[0:chans, pos + 1 : pos + 2]
    for k, value in conv(xs, 0, 6, weights[pos + 1, 0], chans, breadth):
        put_stack(ab, k, gate(softplus(value + offset), k - 1, low, high))
    for k, value in conv(ab, 0, 4, weights[pos + 1, 1], chans, breadth):
        value = mid[:, lanes(k + 2, breadth)] + STEP * value
        if out is None:
            out16[:, lanes(k, breadth)] = value.astype(BF16)
        else:
            out[:, lanes(k, breadth)] = value
            near[:, lanes(k, breadth)] = value.astype(BF16)
            far[:, lanes(k, breadth)] = value.astype(BF16)
    if out is not None:
        put_edges(near, far, 4, even, breadth, [b[:, lanes(k, breadth)] for k in range(4)])


def slope(stack, j, chans, breadth):
    return 1.0 - jnp.exp(-stack[chans : 2 * chans, lanes(j, breadth)].astype(F32))


def single_kernel(pos, skip, base, adjoint, core, chip, hidden, weights, final, outs, e16, bs, es):
    chans, breadth = adjoint.shape[0], adjoint.shape[1] // 4
    even, low, high = place()
    for row in range(-2, 6):
        if 0 <= row < 4:
            value = STEP * adjoint[:, lanes(row, breadth)]
            if final is not None:
                outs[2][:, lanes(row, breadth)] = value.astype(BF16)
        else:
            value = halo_rows(core, chip, even, breadth, row, 2, base)
        put_stack(bs, row + 2, value)
    for k, value in conv(bs, 0, 6, weights[pos, 1], chans, breadth):
        row = k - 1
        value = gate(value * slope(hidden, k + skip, chans, breadth), row, low, high)
        if 0 <= row < 4:
            e16[:, lanes(row, breadth)] = value.astype(BF16)
        put_stack(es, k, value)
    for k, value in conv(es, 0, 4, weights[pos, 0], chans, breadth):
        at = lanes(k, breadth)
        value = adjoint[:, at] + value
        if final is None:
            outs[0][:, at] = value
            outs[1][:, at] = (STEP * value).astype(BF16)
        else:
            value = value.astype(BF16)
            outs[0][:, at] = jnp.where(even_group(), final[:, at], value)
            outs[1][:, at] = jnp.where(even_group(), value, final[:, at])


def even_group():
    return lax.axis_index("depth") % 2 == 0


def double_kernel(pos, adjoint, core, chip, ha, hb, weights, out, near, far, ba16, ea16, bb16, eb16, bs, es, mid):
    chans, breadth = adjoint.shape[0], adjoint.shape[1] // 4
    even, low, high = place()
    for row in range(-4, 8):
        if 0 <= row < 4:
            value = STEP * adjoint[:, lanes(row, breadth)]
            ba16[:, lanes(row, breadth)] = value.astype(BF16)
        else:
            value = halo_rows(core, chip, even, breadth, row)
        put_stack(bs, row + 4, value)
    for k, value in conv(bs, 0, 10, weights[pos, 1], chans, breadth):
        row = k - 3
        value = gate(value * slope(ha, k, chans, breadth), row, low, high)
        if 0 <= row < 4:
            ea16[:, lanes(row, breadth)] = value.astype(BF16)
        put_stack(es, k, value)
    for k, value in conv(es, 0, 8, weights[pos, 0], chans, breadth):
        row = k - 2
        if 0 <= row < 4:
            value = adjoint[:, lanes(row, breadth)] + value
        else:
            value = 4.0 * halo_rows(core, chip, even, breadth, row) + value
        value = gate(value, row, low, high)
        mid[:, lanes(k, breadth)] = value
        value = STEP * value
        if 0 <= row < 4:
            bb16[:, lanes(row, breadth)] = value.astype(BF16)
        put_stack(bs, k, value)
    for k, value in conv(bs, 0, 6, weights[pos - 1, 1], chans, breadth):
        row = k - 1
        value = gate(value * slope(hb, k, chans, breadth), row, low, high)
        if 0 <= row < 4:
            eb16[:, lanes(row, breadth)] = value.astype(BF16)
        put_stack(es, k, value)
    rows = []
    for k, value in conv(es, 0, 4, weights[pos - 1, 0], chans, breadth):
        value = mid[:, lanes(k + 2, breadth)] + value
        out[:, lanes(k, breadth)] = value
        rows.append(STEP * value)
    put_edges(near, far, 0, even, breadth, rows)


def outer(left, right):
    return lax.dot_general(left, right, (((1,), (1,)), ((), ())), preferred_element_type=F32)


def grad_kernel(skip, b, hidden, e, inputs, pay, bd, ed):
    chans, breadth = b.shape[0], b.shape[1] // 4
    for src, dst in ((b, bd), (e, ed)):
        dst[...] = jnp.zeros_like(dst)
        for dy in range(3):
            dst[dy * chans : (dy + 1) * chans, lanes(dy, breadth, 4)] = src[...]
    two = outer(bd[...], hidden[:, lanes(skip, breadth, 6)])
    one = outer(ed[...], inputs[...])
    both = jnp.concatenate([two, one], axis=1)
    for c in range(8):
        for t in range(3):
            pay[c, 24 * t : 24 * t + 24, :] = both[24 * c : 24 * c + 24, 128 * t : 128 * t + 128]
        pay[c, 72:80, :] = jnp.zeros((8, 128), F32)
    ones = jnp.ones((8, e.shape[1]), BF16)
    pay[0, 72:73, 0:chans] = outer(ones, e[...])[0:1]


def packed(total):
    body = total[..., 0:72, :].astype(BF16)
    tail = total[..., 72:80, :]
    bias = tail[..., 0:1, :] + tail[..., 1:2, :]
    head = bias.astype(BF16).astype(F32)
    row = lax.broadcasted_iota(jnp.int32, tail.shape, tail.ndim - 2)
    tail = jnp.where(row == 0, head, jnp.where(row == 1, bias - head, 0.0))
    return body, tail.astype(BF16)


def where_am_i():
    index = lax.axis_index("space")
    return index % 2, (index // 2) % 4, index // 8


def split_kernel(g0, g1, g2, g3, send, keep):
    core, _, _ = where_am_i()
    for k in range(8):
        for at, low, high in ((k, g0, g2), (k + 8, g1, g3)):
            a, b = low[k], high[k]
            keep[at] = jnp.where(core == 0, a, b)
            body, tail = packed(jnp.where(core == 0, b, a))
            send[at, 0:72] = body
            send[at, 72:80] = tail


def spread_kernel(keep_in, part, keep, *sends):
    _, mine, _ = where_am_i()
    for k, dst in enumerate((keep, *sends)):
        for n in range(4):
            at = (mine ^ k) * 4 + n
            total = keep_in[at] + part[at].astype(F32)
            if k == 0:
                dst[n] = total
            else:
                body, tail = packed(total)
                dst[n, 0:72] = body
                dst[n, 72:80] = tail


def total_kernel(own, part1, part2, part3, out):
    for n in range(out.shape[0]):
        pairs = own[n].astype(F32) + part1[n].astype(F32), part2[n].astype(F32) + part3[n].astype(F32)
        body, tail = packed(pairs[0] + pairs[1])
        out[n, 0:72] = body
        out[n, 72:80] = tail


def join_kernel(axis, own, part1, part2, part3, out):
    mine = where_am_i()[axis]
    count = own.shape[0]
    for k, src in enumerate((own, part1, part2, part3)):
        for n in range(count):
            out[(mine ^ k) * count + n] = src[n]


def points_kernel(c, q, pair, far, points, adjoints):
    _, _, height, breadth = c.shape
    group = lax.axis_index("depth")
    first, last = group == 0, group == lax.axis_size("depth") - 1
    for r in range(height):
        at = lanes(r, breadth)
        a, b = pair[:, at].astype(F32), far[:, at].astype(F32)
        points[0, :, r, :] = jnp.where(first, c[0, :, r, :], jnp.where(even_group(), b, a))
        adjoints[0, :, r, :] = jnp.where(last, q[0, :, r, :], jnp.where(even_group(), a, b))


def exit_kernel(scale, own, part, one, two, bias):
    chans = one.shape[1]
    core, _, _ = where_am_i()
    wide = 3 * chans
    for l in range(one.shape[0]):
        base = 8 * (l % 2)

        def piece(k, rows, width=128):
            a, b = own[base + k, rows, 0:width].astype(F32), part[base + k, rows, 0:width].astype(F32)
            return jnp.where(core == l // 2, a, b)

        cols = [
            jnp.concatenate([piece(k, slice(24 * t, 24 * t + 24)) for k in range(8)], axis=0)
            for t in range(3)
        ]
        full = jnp.concatenate(cols, axis=1) * scale
        for dy in range(3):
            rows = full[dy * chans : (dy + 1) * chans]
            two[l, :, dy * wide : (dy + 1) * wide] = rows[:, :wide]
            one[l, :, dy * wide : (dy + 1) * wide] = rows[:, wide:]
        low = piece(0, slice(72, 74), chans)
        bias[l : l + 1, :] = (low[0:1] + low[1:2]) * scale


def call(kernel, outs, args, scratch=(), flops=0):
    size = sum(math.prod(a.shape) * a.dtype.itemsize for a in (*args, *outs))
    return pl.pallas_call(
        kernel,
        out_shape=outs,
        in_specs=[pl.BlockSpec(memory_space=VMEM) for _ in args],
        out_specs=[pl.BlockSpec(memory_space=VMEM) for _ in outs],
        scratch_shapes=list(scratch),
        cost_estimate=pl.CostEstimate(flops=flops, bytes_accessed=size, transcendentals=0),
        compiler_params=pltpu.CompilerParams(vmem_limit_bytes=40 << 20),
    )(*args)


def swaps(near, far):
    count = lax.axis_size("space")
    core = [(i, i ^ 1) for i in range(count)]
    chip = [(i, i + 1 if i % 2 else i - 1) for i in range(1, count - 1)]
    far = lax.ppermute(far, "space", chip)
    near = lax.ppermute(near, "space", core)
    return near, far


def partner(value, mask):
    return lax.ppermute(value, "space", [(i, i ^ mask) for i in range(lax.axis_size("space"))])


def pairs_of_groups(block, first):
    count = lax.axis_size("depth")
    pairs = [(i, i + 1) for i in range(first, count - 1, 2)]
    return lax.ppermute(block, "depth", pairs + [(b, a) for a, b in pairs])


def body(c_points, adjoint_points, conv1_weight, conv2_weight, bias1):
    _, chans, height, breadth = c_points.shape
    layers = conv1_weight.shape[0]
    tiles = lax.axis_size("space")
    scale = 1.0 / math.sqrt(height * tiles * breadth)
    pix = height * breadth
    wide = 3 * chans
    S = jax.ShapeDtypeStruct
    tile32, tile16 = S((chans, pix), F32), S((chans, pix), BF16)
    rows16 = lambda rows: S((chans, rows * breadth), BF16)
    stack = lambda rows: S((wide, rows * breadth), BF16)
    row_flops = 2 * wide * wide * breadth

    s0, s0h = call(entry_kernel, [tile32, tile16], [c_points])
    near1, far1 = swaps(s0h, s0h)
    mats = S((layers, 2, wide, wide), BF16)
    q4, b3, fw, bias = call(
        prepare_kernel, [tile32, tile16, mats, S((128, 8), F32)], [adjoint_points, conv1_weight, conv2_weight, bias1]
    )
    bw = call(turn_kernel, [mats], [conv1_weight, conv2_weight])[0]

    def forward(pos, state, core, chip, last):
        saved = [stack(6), stack(10), stack(6), stack(6)]
        if last:
            outs = [tile16, *saved]
            kernel = lambda st, co, ch, w, b, *rest: forward_kernel(pos, st, co, ch, w, b, None, None, None, None, *rest)
            args = [state, core, chip, fw, bias]
        else:
            outs = [tile32, rows16(6), rows16(6), *saved]

            def kernel(st, co, ch, w, b, edge, out, near, far, *rest):
                forward_kernel(pos, st, co, ch, w, b, edge, out, near, far, None, *rest)

            args = [state, core, chip, fw, bias, b3]
        return call(
            kernel,
            outs,
            args,
            [VMEM((wide, 12 * breadth), BF16), VMEM((chans, 8 * breadth), F32)],
            flops=36 * row_flops,
        )

    s2, near2, far2, x0, a0, x1, a1 = forward(0, s0, near1, far1, False)
    near2, far2 = swaps(near2, far2)
    f16, x2, a2, x3, a3 = forward(2, s2, near2, far2, True)

    def single(pos, skip, base, adjoint, core, chip, hidden, final):
        outs = [tile32, tile16] if final is None else [tile16] * 3
        args = [adjoint, core, chip, hidden, bw]

        def kernel(*refs):
            given, refs = refs[: len(args)], refs[len(args) :]
            held = None if final is None else given[5]
            results, rest = refs[: len(outs)], refs[len(outs) :]
            single_kernel(pos, skip, base, *given[:5], held, results, *rest)

        if final is not None:
            args.append(final)
        return call(
            kernel,
            [*outs, tile16],
            args,
            [VMEM((wide, 8 * breadth), BF16), VMEM((wide, 6 * breadth), BF16)],
            flops=14 * row_flops,
        )

    def grads(skip, b, hidden, e, inputs):
        return call(
            functools.partial(grad_kernel, skip),
            [S((8, 80, 128), F32)],
            [b, hidden, e, inputs],
            [VMEM((wide, 6 * breadth), BF16)] * 2,
            flops=12 * row_flops,
        )[0]

    q3, b2h, e3 = single(3, 0, 4, q4, near2, far2, a3, None)
    near3, far3 = swaps(b2h, b2h)
    g3 = grads(0, b3, a3, e3, x3)
    q1, near4, far4, b2, e2, b1, e1 = call(
        functools.partial(double_kernel, 2),
        [tile32, rows16(2), rows16(2), tile16, tile16, tile16, tile16],
        [q3, near3, far3, a2, a1, bw],
        [VMEM((wide, 12 * breadth), BF16), VMEM((wide, 10 * breadth), BF16), VMEM((chans, 8 * breadth), F32)],
        flops=36 * row_flops,
    )
    near4, far4, g3 = lax.optimization_barrier((near4, far4, g3))
    near4, far4 = swaps(near4, far4)
    g2 = grads(2, b2, a2, e2, x2)
    g1 = grads(0, b1, a1, e1, x1)
    pair, far, b0, e0 = single(0, 2, 0, q1, near4, far4, a0, f16)
    g0 = grads(2, b0, a0, e0, x0)

    def chunks(n, kind):
        return S((n, 80, 128), kind)

    send, keep = call(split_kernel, [chunks(16, BF16), chunks(16, F32)], [g0, g1, g2, g3])
    keep, *sends = call(spread_kernel, [chunks(4, F32)] + [chunks(4, BF16)] * 3, [keep, partner(send, 1)])
    parts = [partner(value, 2 * (k + 1)) for k, value in enumerate(sends)]
    far = pairs_of_groups(far, 1)
    pair = pairs_of_groups(pair, 0)
    mine = call(total_kernel, [chunks(4, BF16)], [keep, *parts])[0]
    parts = [partner(mine, 8 * (k + 1)) for k in range(3)]
    mine = call(total_kernel, [chunks(4, BF16)], [mine, *parts])[0]
    mine, pair, far = lax.optimization_barrier((mine, pair, far))
    parts = [partner(mine, 2 * (k + 1)) for k in range(3)]
    points, adjoints = call(
        points_kernel, [S(c_points.shape, F32), S(c_points.shape, F32)], [c_points, adjoint_points, pair, far]
    )
    mine = call(functools.partial(join_kernel, 1), [chunks(16, BF16)], [mine, *parts])[0]
    mine, points, adjoints = lax.optimization_barrier((mine, points, adjoints))
    grad = S(conv1_weight.shape, F32)
    one, two, vec = call(
        functools.partial(exit_kernel, scale), [grad, grad, S(bias1.shape, F32)], [mine, partner(mine, 1)]
    )
    return points, adjoints, one, two, vec


def solution(mesh):
    in_specs = (
        P("depth", None, "space", None),
        P("depth", None, "space", None),
        P("depth", None, None),
        P("depth", None, None),
        P("depth", None),
    )
    out_specs = in_specs[:2] + (P("depth", None, None), P("depth", None, None), P("depth", None))

    def run(*args):
        return tuple(body(*args))

    return jax.shard_map(run, mesh=mesh, in_specs=in_specs, out_specs=out_specs, check_vma=False)
```

```python
import functools
import math

import jax
import jax.numpy as jnp
from jax import lax
from jax.experimental import pallas as pl
from jax.experimental.pallas import tpu as pltpu
from jax.sharding import PartitionSpec as P


STEP = 0.25
F32 = jnp.float32
BF16 = jnp.bfloat16
VMEM = pltpu.VMEM


def lanes(j, breadth, rows=1):
    return slice(j * breadth, (j + rows) * breadth)


def put_stack(dst, j, row):
    chans, breadth = row.shape
    col = lax.broadcasted_iota(jnp.int32, row.shape, 1)
    left = jnp.where(col == 0, 0.0, pltpu.roll(row, 1, axis=1))
    right = jnp.where(col == breadth - 1, 0.0, pltpu.roll(row, breadth - 1, axis=1))
    dst[0:chans, lanes(j, breadth)] = left.astype(BF16)
    dst[chans : 2 * chans, lanes(j, breadth)] = row.astype(BF16)
    dst[2 * chans : 3 * chans, lanes(j, breadth)] = right.astype(BF16)


def conv(src, first, rows, weight, chans, breadth):
    one = two = None
    for j in range(0, rows + 2, 2):
        both = jnp.dot(weight, src[:, lanes(first + j, breadth, 2)], preferred_element_type=F32)
        for half in range(2):
            z = both[:, lanes(half, breadth)]
            k = j + half - 2
            if k >= 0:
                yield k, two + z[2 * chans :]
            two = one + z[chans : 2 * chans] if one is not None else None
            one = z[:chans]


def even_tile():
    return lax.axis_index("space") % 2 == 0


def halo_rows(core, chip, even, breadth, row, depth=4, base=(0, 0)):
    at = row + depth if row < 0 else row - 4
    near = core[:, lanes(base[0] + at, breadth)]
    far = chip[:, lanes(base[1] + at, breadth)]
    return (jnp.where(even, far, near) if row < 0 else jnp.where(even, near, far)).astype(F32)


def wide_rows(own, core, chip, edge, even, breadth, row):
    if 0 <= row < 4:
        return own[:, lanes(row, breadth)]
    at = row + 8 if row < 0 else row - 4
    far = chip[:, lanes(at, breadth)]
    if row < 0:
        near = edge[:, lanes(at, breadth)] if at < 4 else core[:, lanes(at - 4, breadth)]
        return jnp.where(even, far, near).astype(F32)
    near = core[:, lanes(at, breadth)] if at < 4 else edge[:, lanes(at - 4, breadth)]
    return jnp.where(even, near, far).astype(F32)


def put_edge(dst, base, for_above, rows, breadth):
    for k in range(2):
        value = jnp.where(for_above, rows[k + 2].astype(BF16), rows[k].astype(BF16))
        dst[:, lanes(base + k, breadth)] = value


def gate(value, row):
    index = lax.axis_index("space")
    if row < 0:
        return jnp.where(index >= (3 - row) // 4, value, 0.0)
    if row >= 4:
        return jnp.where(index + row // 4 < lax.axis_size("space"), value, 0.0)
    return value


def softplus(value):
    return jnp.maximum(value, 0.0) + jnp.log1p(jnp.exp(-jnp.abs(value)))


def entry_kernel(field, flat, flat16):
    _, _, height, breadth = field.shape
    for r in range(height):
        at = lanes(r, breadth)
        value = field[0, :, r, :]
        flat[:, at] = value
        flat16[:, at] = value.astype(BF16)


def adjoint_kernel(q, q4, b3):
    _, _, height, breadth = q.shape
    for r in range(height):
        at = lanes(r, breadth)
        value = q[0, :, r, :]
        q4[:, at] = value
        b3[:, at] = (STEP * value).astype(BF16)


def pack_kernel(own, core, b, out):
    even = even_tile()
    breadth = own.shape[1] // 4
    out[:, lanes(0, breadth, 4)] = jnp.where(even, own[...], core[...])
    out[:, lanes(4, breadth, 4)] = jnp.where(even, core[...], own[...])
    put_edge(out, 8, jnp.logical_not(even), [b[:, lanes(k, breadth)] for k in range(4)], breadth)


def pass_kernel(chip, b, out):
    even = even_tile()
    breadth = b.shape[1] // 4
    out[:, lanes(0, breadth, 4)] = jnp.where(even, chip[:, lanes(4, breadth, 4)], chip[:, lanes(0, breadth, 4)])
    put_edge(out, 4, even, [b[:, lanes(k, breadth)] for k in range(4)], breadth)


def prepare_kernel(w1, w2, bias, forward, columns):
    layers, chans, _ = w1.shape
    wide = 3 * chans
    for l in range(layers):
        for which, w in enumerate((w1, w2)):
            for dy in range(3):
                forward[l, which, dy * chans : (dy + 1) * chans, :] = w[l, :, dy * wide : (dy + 1) * wide]
    rows = jnp.concatenate([bias[...], jnp.zeros((8 - layers, chans), F32)], axis=0)
    columns[...] = jnp.concatenate([rows, jnp.zeros((8, 128 - chans), F32)], axis=1).T


def turn_kernel(w1, w2, backward):
    layers, chans, _ = w1.shape
    for l in range(layers):
        for which, w in enumerate((w1, w2)):
            turned = w[l].astype(F32).T
            for e in range(3):
                blocks = [turned[(8 - 3 * e - s) * chans : (9 - 3 * e - s) * chans] for s in range(3)]
                backward[l, which, e * chans : (e + 1) * chans, :] = jnp.concatenate(blocks, axis=1).astype(BF16)


def forward_kernel(state, core, chip, edge, weights, bias, out, *refs):
    inputs, hidden, (xs, wide_a, mid) = refs[0:4], refs[4:8], refs[8:]
    chans, breadth = state.shape[0], state.shape[1] // 4
    even = even_tile()
    start = functools.partial(wide_rows, state, core, chip, edge, even, breadth)
    for row in range(-8, 12):
        put_stack(xs, row + 8, start(row))
    for pos in range(4):
        reach = 8 - 2 * pos
        inputs[pos][...] = xs[:, lanes(reach - 1, breadth, 6)]
        offset = bias[0:chans, pos : pos + 1]
        dst = wide_a if pos < 2 else hidden[pos]
        for k, value in conv(xs, 0, 2 + 2 * reach, weights[pos, 0], chans, breadth):
            put_stack(dst, k, gate(softplus(value + offset), k + 1 - reach))
        if pos < 2:
            hidden[pos][...] = dst[:, lanes(reach - 2, breadth, 6)]
        for k, value in conv(dst, 0, 2 * reach, weights[pos, 1], chans, breadth):
            row = k + 2 - reach
            at = lanes(row + 6, breadth)
            value = (mid[:, at] if pos else start(row)) + STEP * value
            if pos == 3:
                out[:, lanes(row, breadth)] = value.astype(BF16)
            else:
                value = gate(value, row)
                put_stack(xs, k, value)
                mid[:, at] = value


def slope(stack, j, chans, breadth):
    return 1.0 - jnp.exp(-stack[chans : 2 * chans, lanes(j, breadth)].astype(F32))


def single_kernel(pos, skip, base, adjoint, core, chip, hidden, weights, final, outs, e16, bs, es):
    chans, breadth = adjoint.shape[0], adjoint.shape[1] // 4
    even = even_tile()
    for row in range(-2, 6):
        if 0 <= row < 4:
            value = STEP * adjoint[:, lanes(row, breadth)]
            if final is not None:
                outs[2][:, lanes(row, breadth)] = value.astype(BF16)
        else:
            value = halo_rows(core, chip, even, breadth, row, 2, base)
        put_stack(bs, row + 2, value)
    for k, value in conv(bs, 0, 6, weights[pos, 1], chans, breadth):
        row = k - 1
        value = gate(value * slope(hidden, k + skip, chans, breadth), row)
        if 0 <= row < 4:
            e16[:, lanes(row, breadth)] = value.astype(BF16)
        put_stack(es, k, value)
    for k, value in conv(es, 0, 4, weights[pos, 0], chans, breadth):
        at = lanes(k, breadth)
        value = adjoint[:, at] + value
        if final is None:
            outs[0][:, at] = value
            outs[1][:, at] = (STEP * value).astype(BF16)
        else:
            value = value.astype(BF16)
            outs[0][:, at] = jnp.where(even_group(), final[:, at], value)
            outs[1][:, at] = jnp.where(even_group(), value, final[:, at])


def even_group():
    return lax.axis_index("depth") % 2 == 0


def double_kernel(pos, adjoint, core, chip, ha, hb, weights, out, near, far, ba16, ea16, bb16, eb16, bs, es, mid):
    chans, breadth = adjoint.shape[0], adjoint.shape[1] // 4
    even = even_tile()
    for row in range(-4, 8):
        if 0 <= row < 4:
            value = STEP * adjoint[:, lanes(row, breadth)]
            ba16[:, lanes(row, breadth)] = value.astype(BF16)
        else:
            value = halo_rows(core, chip, even, breadth, row)
        put_stack(bs, row + 4, value)
    for k, value in conv(bs, 0, 10, weights[pos, 1], chans, breadth):
        row = k - 3
        value = gate(value * slope(ha, k, chans, breadth), row)
        if 0 <= row < 4:
            ea16[:, lanes(row, breadth)] = value.astype(BF16)
        put_stack(es, k, value)
    for k, value in conv(es, 0, 8, weights[pos, 0], chans, breadth):
        row = k - 2
        if 0 <= row < 4:
            value = adjoint[:, lanes(row, breadth)] + value
        else:
            value = 4.0 * halo_rows(core, chip, even, breadth, row) + value
        value = gate(value, row)
        mid[:, lanes(k, breadth)] = value
        value = STEP * value
        if 0 <= row < 4:
            bb16[:, lanes(row, breadth)] = value.astype(BF16)
        put_stack(bs, k, value)
    for k, value in conv(bs, 0, 6, weights[pos - 1, 1], chans, breadth):
        row = k - 1
        value = gate(value * slope(hb, k, chans, breadth), row)
        if 0 <= row < 4:
            eb16[:, lanes(row, breadth)] = value.astype(BF16)
        put_stack(es, k, value)
    rows = []
    for k, value in conv(es, 0, 4, weights[pos - 1, 0], chans, breadth):
        value = mid[:, lanes(k + 2, breadth)] + value
        out[:, lanes(k, breadth)] = value
        rows.append(STEP * value)
    put_edge(near, 0, even, rows, breadth)
    put_edge(far, 0, jnp.logical_not(even), rows, breadth)


def outer(left, right):
    return lax.dot_general(left, right, (((1,), (1,)), ((), ())), preferred_element_type=F32)


def grad_kernel(skip, b, hidden, e, inputs, pay, bd, ed):
    chans, breadth = b.shape[0], b.shape[1] // 4
    for src, dst in ((b, bd), (e, ed)):
        dst[...] = jnp.zeros_like(dst)
        for dy in range(3):
            dst[dy * chans : (dy + 1) * chans, lanes(dy, breadth, 4)] = src[...]
    two = outer(bd[...], hidden[:, lanes(skip, breadth, 6)])
    one = outer(ed[...], inputs[...])
    both = jnp.concatenate([two, one], axis=1)
    for c in range(8):
        for t in range(3):
            pay[c, 24 * t : 24 * t + 24, :] = both[24 * c : 24 * c + 24, 128 * t : 128 * t + 128]
        pay[c, 72:80, :] = jnp.zeros((8, 128), F32)
    ones = jnp.ones((8, e.shape[1]), BF16)
    pay[0, 72:73, 0:chans] = outer(ones, e[...])[0:1]


def packed(total):
    body = total[..., 0:72, :].astype(BF16)
    tail = total[..., 72:80, :]
    bias = tail[..., 0:1, :] + tail[..., 1:2, :]
    head = bias.astype(BF16).astype(F32)
    row = lax.broadcasted_iota(jnp.int32, tail.shape, tail.ndim - 2)
    tail = jnp.where(row == 0, head, jnp.where(row == 1, bias - head, 0.0))
    return body, tail.astype(BF16)


def where_am_i():
    index = lax.axis_index("space")
    return index % 2, (index // 2) % 4, index // 8


def split_kernel(g0, g1, g2, g3, send, keep):
    core, _, _ = where_am_i()
    for k in range(8):
        for at, low, high in ((k, g0, g2), (k + 8, g1, g3)):
            a, b = low[k], high[k]
            keep[at] = jnp.where(core == 0, a, b)
            body, tail = packed(jnp.where(core == 0, b, a))
            send[at, 0:72] = body
            send[at, 72:80] = tail


def spread_kernel(keep_in, part, keep, *sends):
    _, mine, _ = where_am_i()
    for k, dst in enumerate((keep, *sends)):
        for n in range(4):
            at = (mine ^ k) * 4 + n
            total = keep_in[at] + part[at].astype(F32)
            if k == 0:
                dst[n] = total
            else:
                body, tail = packed(total)
                dst[n, 0:72] = body
                dst[n, 72:80] = tail


def total_kernel(own, part1, part2, part3, out):
    for n in range(out.shape[0]):
        pairs = own[n].astype(F32) + part1[n].astype(F32), part2[n].astype(F32) + part3[n].astype(F32)
        body, tail = packed(pairs[0] + pairs[1])
        out[n, 0:72] = body
        out[n, 72:80] = tail


def join_kernel(axis, own, part1, part2, part3, out):
    mine = where_am_i()[axis]
    count = own.shape[0]
    for k, src in enumerate((own, part1, part2, part3)):
        for n in range(count):
            out[(mine ^ k) * count + n] = src[n]


def points_kernel(c, q, pair, far, points, adjoints):
    _, _, height, breadth = c.shape
    group = lax.axis_index("depth")
    first, last = group == 0, group == lax.axis_size("depth") - 1
    for r in range(height):
        at = lanes(r, breadth)
        a, b = pair[:, at].astype(F32), far[:, at].astype(F32)
        points[0, :, r, :] = jnp.where(first, c[0, :, r, :], jnp.where(even_group(), b, a))
        adjoints[0, :, r, :] = jnp.where(last, q[0, :, r, :], jnp.where(even_group(), a, b))


def exit_kernel(scale, own, part, one, two, bias):
    chans = one.shape[1]
    core, _, _ = where_am_i()
    wide = 3 * chans
    for l in range(one.shape[0]):
        base = 8 * (l % 2)

        def piece(k, rows, width=128):
            a, b = own[base + k, rows, 0:width].astype(F32), part[base + k, rows, 0:width].astype(F32)
            return jnp.where(core == l // 2, a, b)

        cols = [
            jnp.concatenate([piece(k, slice(24 * t, 24 * t + 24)) for k in range(8)], axis=0)
            for t in range(3)
        ]
        full = jnp.concatenate(cols, axis=1) * scale
        for dy in range(3):
            rows = full[dy * chans : (dy + 1) * chans]
            two[l, :, dy * wide : (dy + 1) * wide] = rows[:, :wide]
            one[l, :, dy * wide : (dy + 1) * wide] = rows[:, wide:]
        low = piece(0, slice(72, 74), chans)
        bias[l : l + 1, :] = (low[0:1] + low[1:2]) * scale


def call(kernel, outs, args, scratch=(), flops=0):
    size = sum(math.prod(a.shape) * a.dtype.itemsize for a in (*args, *outs))
    return pl.pallas_call(
        kernel,
        out_shape=outs,
        in_specs=[pl.BlockSpec(memory_space=VMEM) for _ in args],
        out_specs=[pl.BlockSpec(memory_space=VMEM) for _ in outs],
        scratch_shapes=list(scratch),
        cost_estimate=pl.CostEstimate(flops=flops, bytes_accessed=size, transcendentals=0),
        compiler_params=pltpu.CompilerParams(vmem_limit_bytes=40 << 20),
    )(*args)


def swap_cores(value):
    return lax.ppermute(value, "space", [(i, i ^ 1) for i in range(lax.axis_size("space"))])


def swap_chips(value):
    count = lax.axis_size("space")
    return lax.ppermute(value, "space", [(i, i + 1 if i % 2 else i - 1) for i in range(1, count - 1)])


def swaps(near, far):
    far = swap_chips(far)
    return swap_cores(near), far


def partner(value, mask):
    return lax.ppermute(value, "space", [(i, i ^ mask) for i in range(lax.axis_size("space"))])


def pairs_of_groups(block, first):
    count = lax.axis_size("depth")
    pairs = [(i, i + 1) for i in range(first, count - 1, 2)]
    return lax.ppermute(block, "depth", pairs + [(b, a) for a, b in pairs])


def body(c_points, adjoint_points, conv1_weight, conv2_weight, bias1):
    _, chans, height, breadth = c_points.shape
    layers = conv1_weight.shape[0]
    tiles = lax.axis_size("space")
    scale = 1.0 / math.sqrt(height * tiles * breadth)
    pix = height * breadth
    wide = 3 * chans
    S = jax.ShapeDtypeStruct
    tile32, tile16 = S((chans, pix), F32), S((chans, pix), BF16)
    rows16 = lambda rows: S((chans, rows * breadth), BF16)
    stack = lambda rows: S((wide, rows * breadth), BF16)
    row_flops = 2 * wide * wide * breadth

    s0, s0h = call(entry_kernel, [tile32, tile16], [c_points])
    near1 = swap_cores(s0h)
    q4, b3 = call(adjoint_kernel, [tile32, tile16], [adjoint_points])
    far1 = swap_chips(call(pack_kernel, [rows16(10)], [s0h, near1, b3])[0])
    mats = S((layers, 2, wide, wide), BF16)
    fw, bias = call(prepare_kernel, [mats, S((128, 8), F32)], [conv1_weight, conv2_weight, bias1])
    bw = call(turn_kernel, [mats], [conv1_weight, conv2_weight])[0]
    far1, fw, bias, bw = lax.optimization_barrier((far1, fw, bias, bw))
    near2 = swap_cores(call(pass_kernel, [rows16(6)], [far1, b3])[0])
    f16, x0, x1, x2, x3, a0, a1, a2, a3 = call(
        forward_kernel,
        [tile16, *[stack(6)] * 4, stack(6), stack(6), stack(10), stack(6)],
        [s0, near1, far1, near2, fw, bias],
        [VMEM((wide, 20 * breadth), BF16), VMEM((wide, 18 * breadth), BF16), VMEM((chans, 16 * breadth), F32)],
        flops=104 * row_flops,
    )

    def single(pos, skip, base, adjoint, core, chip, hidden, final):
        outs = [tile32, tile16] if final is None else [tile16] * 3
        args = [adjoint, core, chip, hidden, bw]

        def kernel(*refs):
            given, refs = refs[: len(args)], refs[len(args) :]
            held = None if final is None else given[5]
            results, rest = refs[: len(outs)], refs[len(outs) :]
            single_kernel(pos, skip, base, *given[:5], held, results, *rest)

        if final is not None:
            args.append(final)
        return call(
            kernel,
            [*outs, tile16],
            args,
            [VMEM((wide, 8 * breadth), BF16), VMEM((wide, 6 * breadth), BF16)],
            flops=14 * row_flops,
        )

    def grads(skip, b, hidden, e, inputs):
        return call(
            functools.partial(grad_kernel, skip),
            [S((8, 80, 128), F32)],
            [b, hidden, e, inputs],
            [VMEM((wide, 6 * breadth), BF16)] * 2,
            flops=12 * row_flops,
        )[0]

    q3, b2h, e3 = single(3, 0, (4, 8), q4, near2, far1, a3, None)
    near3, far3 = swaps(b2h, b2h)
    g3 = grads(0, b3, a3, e3, x3)
    q1, near4, far4, b2, e2, b1, e1 = call(
        functools.partial(double_kernel, 2),
        [tile32, rows16(2), rows16(2), tile16, tile16, tile16, tile16],
        [q3, near3, far3, a2, a1, bw],
        [VMEM((wide, 12 * breadth), BF16), VMEM((wide, 10 * breadth), BF16), VMEM((chans, 8 * breadth), F32)],
        flops=36 * row_flops,
    )
    near4, far4, g3 = lax.optimization_barrier((near4, far4, g3))
    near4, far4 = swaps(near4, far4)
    g2 = grads(2, b2, a2, e2, x2)
    g1 = grads(0, b1, a1, e1, x1)
    pair, far, b0, e0 = single(0, 0, (0, 0), q1, near4, far4, a0, f16)
    g0 = grads(0, b0, a0, e0, x0)

    def chunks(n, kind):
        return S((n, 80, 128), kind)

    send, keep = call(split_kernel, [chunks(16, BF16), chunks(16, F32)], [g0, g1, g2, g3])
    keep, *sends = call(spread_kernel, [chunks(4, F32)] + [chunks(4, BF16)] * 3, [keep, partner(send, 1)])
    parts = [partner(value, 2 * (k + 1)) for k, value in enumerate(sends)]
    far = pairs_of_groups(far, 1)
    pair = pairs_of_groups(pair, 0)
    mine = call(total_kernel, [chunks(4, BF16)], [keep, *parts])[0]
    parts = [partner(mine, 8 * (k + 1)) for k in range(3)]
    mine = call(total_kernel, [chunks(4, BF16)], [mine, *parts])[0]
    mine, pair, far = lax.optimization_barrier((mine, pair, far))
    parts = [partner(mine, 2 * (k + 1)) for k in range(3)]
    points, adjoints = call(
        points_kernel, [S(c_points.shape, F32), S(c_points.shape, F32)], [c_points, adjoint_points, pair, far]
    )
    mine = call(functools.partial(join_kernel, 1), [chunks(16, BF16)], [mine, *parts])[0]
    mine, points, adjoints = lax.optimization_barrier((mine, points, adjoints))
    grad = S(conv1_weight.shape, F32)
    one, two, vec = call(
        functools.partial(exit_kernel, scale), [grad, grad, S(bias1.shape, F32)], [mine, partner(mine, 1)]
    )
    return points, adjoints, one, two, vec


def solution(mesh):
    in_specs = (
        P("depth", None, "space", None),
        P("depth", None, "space", None),
        P("depth", None, None),
        P("depth", None, None),
        P("depth", None),
    )
    out_specs = in_specs[:2] + (P("depth", None, None), P("depth", None, None), P("depth", None))

    def run(*args):
        return tuple(body(*args))

    return jax.shard_map(run, mesh=mesh, in_specs=in_specs, out_specs=out_specs, check_vma=False)
```

```python
import functools
import math

import jax
import jax.numpy as jnp
from jax import lax
from jax.experimental import pallas as pl
from jax.experimental.pallas import tpu as pltpu
from jax.sharding import PartitionSpec as P


STEP = 0.25
F32 = jnp.float32
BF16 = jnp.bfloat16
VMEM = pltpu.VMEM


def lanes(j, breadth, rows=1):
    return slice(j * breadth, (j + rows) * breadth)


def put_stack(dst, j, row):
    chans, breadth = row.shape
    row = row.astype(BF16)
    col = lax.broadcasted_iota(jnp.int32, row.shape, 1)
    none = jnp.zeros((), BF16)
    left = jnp.where(col == 0, none, pltpu.roll(row, 1, axis=1))
    right = jnp.where(col == breadth - 1, none, pltpu.roll(row, breadth - 1, axis=1))
    dst[0:chans, lanes(j, breadth)] = left
    dst[chans : 2 * chans, lanes(j, breadth)] = row
    dst[2 * chans : 3 * chans, lanes(j, breadth)] = right


def conv(src, first, rows, weight, chans, breadth):
    one = two = None
    for j in range(0, rows + 2, 2):
        both = jnp.dot(weight, src[:, lanes(first + j, breadth, 2)], preferred_element_type=F32)
        for half in range(2):
            z = both[:, lanes(half, breadth)]
            k = j + half - 2
            if k >= 0:
                yield k, two + z[2 * chans :]
            two = one + z[chans : 2 * chans] if one is not None else None
            one = z[:chans]


def even_tile():
    return lax.axis_index("space") % 2 == 0


def halo_rows(core, chip, even, breadth, row, depth=4, base=(0, 0)):
    at = row + depth if row < 0 else row - 4
    near = core[:, lanes(base[0] + at, breadth)]
    far = chip[:, lanes(base[1] + at, breadth)]
    return (jnp.where(even, far, near) if row < 0 else jnp.where(even, near, far)).astype(F32)


def wide_rows(own, core, chip, edge, even, breadth, row):
    if 0 <= row < 4:
        return own[:, lanes(row, breadth)]
    at = row + 8 if row < 0 else row - 4
    far = chip[:, lanes(at, breadth)]
    if row < 0:
        near = edge[:, lanes(at, breadth)] if at < 4 else core[:, lanes(at - 4, breadth)]
        return jnp.where(even, far, near).astype(F32)
    near = core[:, lanes(at, breadth)] if at < 4 else edge[:, lanes(at - 4, breadth)]
    return jnp.where(even, near, far).astype(F32)


def put_edge(dst, base, for_above, rows, breadth):
    for k in range(2):
        value = jnp.where(for_above, rows[k + 2].astype(BF16), rows[k].astype(BF16))
        dst[:, lanes(base + k, breadth)] = value


def gate(value, row):
    index = lax.axis_index("space")
    if row < 0:
        return jnp.where(index >= (3 - row) // 4, value, 0.0)
    if row >= 4:
        return jnp.where(index + row // 4 < lax.axis_size("space"), value, 0.0)
    return value


def softplus(value):
    return jnp.maximum(value, 0.0) + jnp.log1p(jnp.exp(-jnp.abs(value)))


def entry_kernel(field, flat, flat16):
    _, _, height, breadth = field.shape
    for r in range(height):
        at = lanes(r, breadth)
        value = field[0, :, r, :]
        flat[:, at] = value
        flat16[:, at] = value.astype(BF16)


def adjoint_kernel(q, q4, b3):
    _, _, height, breadth = q.shape
    for r in range(height):
        at = lanes(r, breadth)
        value = q[0, :, r, :]
        q4[:, at] = value
        b3[:, at] = (STEP * value).astype(BF16)


def pack_kernel(own, core, b, out):
    even = even_tile()
    breadth = own.shape[1] // 4
    out[:, lanes(0, breadth, 4)] = jnp.where(even, own[...], core[...])
    out[:, lanes(4, breadth, 4)] = jnp.where(even, core[...], own[...])
    put_edge(out, 8, jnp.logical_not(even), [b[:, lanes(k, breadth)] for k in range(4)], breadth)


def pass_kernel(chip, b, out):
    even = even_tile()
    breadth = b.shape[1] // 4
    out[:, lanes(0, breadth, 4)] = jnp.where(even, chip[:, lanes(4, breadth, 4)], chip[:, lanes(0, breadth, 4)])
    put_edge(out, 4, even, [b[:, lanes(k, breadth)] for k in range(4)], breadth)


def prepare_kernel(w1, w2, bias, forward, columns):
    layers, chans, _ = w1.shape
    wide = 3 * chans
    for l in range(layers):
        for which, w in enumerate((w1, w2)):
            for dy in range(3):
                forward[l, which, dy * chans : (dy + 1) * chans, :] = w[l, :, dy * wide : (dy + 1) * wide]
    rows = jnp.concatenate([bias[...], jnp.zeros((8 - layers, chans), F32)], axis=0)
    columns[...] = jnp.concatenate([rows, jnp.zeros((8, 128 - chans), F32)], axis=1).T


def turn_kernel(w1, w2, backward):
    layers, chans, _ = w1.shape
    for l in range(layers):
        for which, w in enumerate((w1, w2)):
            turned = w[l].astype(F32).T
            for e in range(3):
                blocks = [turned[(8 - 3 * e - s) * chans : (9 - 3 * e - s) * chans] for s in range(3)]
                backward[l, which, e * chans : (e + 1) * chans, :] = jnp.concatenate(blocks, axis=1).astype(BF16)


def forward_kernel(state, core, chip, edge, weights, bias, out, *refs):
    inputs, hidden, (xs, wide_a, mid) = refs[0:4], refs[4:8], refs[8:]
    chans, breadth = state.shape[0], state.shape[1] // 4
    even = even_tile()
    start = functools.partial(wide_rows, state, core, chip, edge, even, breadth)
    for row in range(-8, 12):
        put_stack(xs, row + 8, start(row))
    for pos in range(4):
        reach = 8 - 2 * pos
        inputs[pos][...] = xs[:, lanes(reach - 1, breadth, 6)]
        offset = bias[0:chans, pos : pos + 1]
        dst = wide_a if pos < 2 else hidden[pos]
        for k, value in conv(xs, 0, 2 + 2 * reach, weights[pos, 0], chans, breadth):
            put_stack(dst, k, gate(softplus(value + offset), k + 1 - reach))
        if pos < 2:
            hidden[pos][...] = dst[:, lanes(reach - 2, breadth, 6)]
        for k, value in conv(dst, 0, 2 * reach, weights[pos, 1], chans, breadth):
            row = k + 2 - reach
            at = lanes(row + 6, breadth)
            value = (mid[:, at] if pos else start(row)) + STEP * value
            if pos == 3:
                out[:, lanes(row, breadth)] = value.astype(BF16)
            else:
                value = gate(value, row)
                put_stack(xs, k, value)
                mid[:, at] = value


def slope(stack, j, chans, breadth):
    return 1.0 - jnp.exp(-stack[chans : 2 * chans, lanes(j, breadth)].astype(F32))


def single_kernel(pos, skip, base, adjoint, core, chip, hidden, weights, final, outs, e16, bs, es):
    chans, breadth = adjoint.shape[0], adjoint.shape[1] // 4
    even = even_tile()
    for row in range(-2, 6):
        if 0 <= row < 4:
            value = STEP * adjoint[:, lanes(row, breadth)]
            if final is not None:
                outs[2][:, lanes(row, breadth)] = value.astype(BF16)
        else:
            value = halo_rows(core, chip, even, breadth, row, 2, base)
        put_stack(bs, row + 2, value)
    for k, value in conv(bs, 0, 6, weights[pos, 1], chans, breadth):
        row = k - 1
        value = gate(value * slope(hidden, k + skip, chans, breadth), row)
        if 0 <= row < 4:
            e16[:, lanes(row, breadth)] = value.astype(BF16)
        put_stack(es, k, value)
    for k, value in conv(es, 0, 4, weights[pos, 0], chans, breadth):
        at = lanes(k, breadth)
        value = adjoint[:, at] + value
        if final is None:
            outs[0][:, at] = value
            outs[1][:, at] = (STEP * value).astype(BF16)
        else:
            value = value.astype(BF16)
            outs[0][:, at] = jnp.where(even_group(), final[:, at], value)
            outs[1][:, at] = jnp.where(even_group(), value, final[:, at])


def even_group():
    return lax.axis_index("depth") % 2 == 0


def double_kernel(pos, adjoint, core, chip, ha, hb, weights, out, near, far, ba16, ea16, bb16, eb16, bs, es, mid):
    chans, breadth = adjoint.shape[0], adjoint.shape[1] // 4
    even = even_tile()
    for row in range(-4, 8):
        if 0 <= row < 4:
            value = STEP * adjoint[:, lanes(row, breadth)]
            ba16[:, lanes(row, breadth)] = value.astype(BF16)
        else:
            value = halo_rows(core, chip, even, breadth, row)
        put_stack(bs, row + 4, value)
    for k, value in conv(bs, 0, 10, weights[pos, 1], chans, breadth):
        row = k - 3
        value = gate(value * slope(ha, k, chans, breadth), row)
        if 0 <= row < 4:
            ea16[:, lanes(row, breadth)] = value.astype(BF16)
        put_stack(es, k, value)
    for k, value in conv(es, 0, 8, weights[pos, 0], chans, breadth):
        row = k - 2
        if 0 <= row < 4:
            value = adjoint[:, lanes(row, breadth)] + value
        else:
            value = 4.0 * halo_rows(core, chip, even, breadth, row) + value
        value = gate(value, row)
        mid[:, lanes(k, breadth)] = value
        value = STEP * value
        if 0 <= row < 4:
            bb16[:, lanes(row, breadth)] = value.astype(BF16)
        put_stack(bs, k, value)
    for k, value in conv(bs, 0, 6, weights[pos - 1, 1], chans, breadth):
        row = k - 1
        value = gate(value * slope(hb, k, chans, breadth), row)
        if 0 <= row < 4:
            eb16[:, lanes(row, breadth)] = value.astype(BF16)
        put_stack(es, k, value)
    rows = []
    for k, value in conv(es, 0, 4, weights[pos - 1, 0], chans, breadth):
        value = mid[:, lanes(k + 2, breadth)] + value
        out[:, lanes(k, breadth)] = value
        rows.append(STEP * value)
    put_edge(near, 0, even, rows, breadth)
    put_edge(far, 0, jnp.logical_not(even), rows, breadth)


def outer(left, right):
    return lax.dot_general(left, right, (((1,), (1,)), ((), ())), preferred_element_type=F32)


CHUNK = 4 * 72 + 8


def grad_kernel(skip, b, hidden, e, inputs, pay, bd, ed):
    chans, breadth = b.shape[0], b.shape[1] // 4
    for src, dst in ((b, bd), (e, ed)):
        dst[...] = jnp.zeros_like(dst)
        for dy in range(3):
            dst[dy * chans : (dy + 1) * chans, lanes(dy, breadth, 4)] = src[...]
    two = outer(bd[...], hidden[:, lanes(skip, breadth, 6)])
    one = outer(ed[...], inputs[...])
    both = jnp.concatenate([two, one], axis=1)
    for c in range(8):
        for t in range(3):
            at = 72 * (c % 4) + 24 * t
            pay[c // 4, at : at + 24, :] = both[24 * c : 24 * c + 24, 128 * t : 128 * t + 128]
    for c in range(2):
        pay[c, 288:CHUNK, :] = jnp.zeros((8, 128), F32)
    ones = jnp.ones((8, e.shape[1]), BF16)
    pay[0, 288:289, 0:chans] = outer(ones, e[...])[0:1]


def put_packed(dst, at, total):
    tail = total[288:CHUNK]
    bias = tail[0:1] + tail[1:2]
    head = bias.astype(BF16).astype(F32)
    row = lax.broadcasted_iota(jnp.int32, tail.shape, 0)
    tail = jnp.where(row == 0, head, jnp.where(row == 1, bias - head, 0.0))
    dst[at, 0:288] = total[0:288].astype(BF16)
    dst[at, 288:CHUNK] = tail.astype(BF16)


def where_am_i():
    index = lax.axis_index("space")
    return index % 2, (index // 2) % 4, index // 8


def split_kernel(g0, g1, g2, g3, send, keep):
    core, _, _ = where_am_i()
    for k in range(2):
        for at, low, high in ((k, g0, g2), (k + 2, g1, g3)):
            a, b = low[k], high[k]
            keep[at] = jnp.where(core == 0, a, b)
            put_packed(send, at, jnp.where(core == 0, b, a))


def spread_kernel(keep_in, part, keep, *sends):
    _, mine, _ = where_am_i()
    for k, dst in enumerate((keep, *sends)):
        total = keep_in[mine ^ k] + part[mine ^ k].astype(F32)
        if k == 0:
            dst[0] = total
        else:
            put_packed(dst, 0, total)


def total_kernel(own, part1, part2, part3, out):
    pairs = own[0].astype(F32) + part1[0].astype(F32), part2[0].astype(F32) + part3[0].astype(F32)
    put_packed(out, 0, pairs[0] + pairs[1])


def join_kernel(own, part1, part2, part3, out):
    _, mine, _ = where_am_i()
    for k, src in enumerate((own, part1, part2, part3)):
        out[mine ^ k] = src[0]


def points_kernel(c, q, pair, far, points, adjoints):
    _, _, height, breadth = c.shape
    group = lax.axis_index("depth")
    first, last = group == 0, group == lax.axis_size("depth") - 1
    for r in range(height):
        at = lanes(r, breadth)
        a, b = pair[:, at].astype(F32), far[:, at].astype(F32)
        points[0, :, r, :] = jnp.where(first, c[0, :, r, :], jnp.where(even_group(), b, a))
        adjoints[0, :, r, :] = jnp.where(last, q[0, :, r, :], jnp.where(even_group(), a, b))


def lay_out(scale, src, base, one, two, wide_one, wide_two, sems):
    chans = wide_one.shape[1]
    wide = 3 * chans
    copies = []
    for l in range(2):
        cols = []
        for t in range(3):
            at = [(2 * l + k // 4, 72 * (k % 4) + 24 * t) for k in range(8)]
            cols.append(jnp.concatenate([src[c, r : r + 24, :].astype(F32) for c, r in at], axis=0))
        full = jnp.concatenate(cols, axis=1) * scale
        for dy in range(3):
            rows = full[dy * chans : (dy + 1) * chans]
            wide_two[l, :, dy * wide : (dy + 1) * wide] = rows[:, :wide]
            wide_one[l, :, dy * wide : (dy + 1) * wide] = rows[:, wide:]
        for k, (held, out) in enumerate(((wide_one, one), (wide_two, two))):
            copy = pltpu.make_async_copy(held.at[l], out.at[base + l], sems.at[2 * l + k])
            copy.start()
            copies.append(copy)
    return copies


def exit_own_kernel(scale, own, one, two, wide_one, wide_two, sems):
    core, _, _ = where_am_i()
    for copy in lay_out(scale, own, 2 * core, one, two, wide_one, wide_two, sems):
        copy.wait()


def exit_other_kernel(scale, part, own, _one, _two, one, two, bias, wide_one, wide_two, sems, vec, sem):
    core, _, _ = where_am_i()
    chans = vec.shape[1]
    for l in range(vec.shape[0]):
        at = (2 * (l % 2), slice(288, 290), slice(0, chans))
        low = jnp.where(core == l // 2, own[at].astype(F32), part[at].astype(F32))
        vec[l : l + 1, :] = (low[0:1] + low[1:2]) * scale
    last = pltpu.make_async_copy(vec, bias, sem)
    last.start()
    for copy in lay_out(scale, part, 2 * (1 - core), one, two, wide_one, wide_two, sems):
        copy.wait()
    last.wait()


def exit_calls(scale, mine, part, grad, vec):
    _, chans, wide = grad.shape
    hbm = pl.BlockSpec(memory_space=pl.ANY)
    near = pl.BlockSpec(memory_space=VMEM)
    scratch = [VMEM((2, chans, wide), F32)] * 2 + [pltpu.SemaphoreType.DMA((4,))]
    options = dict(
        cost_estimate=pl.CostEstimate(flops=0, bytes_accessed=16 * chans * wide, transcendentals=0),
        compiler_params=pltpu.CompilerParams(vmem_limit_bytes=40 << 20),
    )
    held = pl.pallas_call(
        functools.partial(exit_own_kernel, scale),
        out_shape=[grad, grad],
        in_specs=[near],
        out_specs=[hbm, hbm],
        scratch_shapes=scratch,
        name="exit_own",
        **options,
    )(mine)
    return pl.pallas_call(
        functools.partial(exit_other_kernel, scale),
        out_shape=[grad, grad, vec],
        in_specs=[near, near, hbm, hbm],
        out_specs=[hbm, hbm, hbm],
        scratch_shapes=[*scratch, VMEM(vec.shape, F32), pltpu.SemaphoreType.DMA],
        input_output_aliases={2: 0, 3: 1},
        name="exit_other",
        **options,
    )(part, mine, *held)


def call(kernel, outs, args, scratch=(), flops=0):
    size = sum(math.prod(a.shape) * a.dtype.itemsize for a in (*args, *outs))
    return pl.pallas_call(
        kernel,
        out_shape=outs,
        in_specs=[pl.BlockSpec(memory_space=VMEM) for _ in args],
        out_specs=[pl.BlockSpec(memory_space=VMEM) for _ in outs],
        scratch_shapes=list(scratch),
        cost_estimate=pl.CostEstimate(flops=flops, bytes_accessed=size, transcendentals=0),
        compiler_params=pltpu.CompilerParams(vmem_limit_bytes=40 << 20),
    )(*args)


def swap_cores(value):
    return lax.ppermute(value, "space", [(i, i ^ 1) for i in range(lax.axis_size("space"))])


def swap_chips(value):
    count = lax.axis_size("space")
    return lax.ppermute(value, "space", [(i, i + 1 if i % 2 else i - 1) for i in range(1, count - 1)])


def swaps(near, far):
    far = swap_chips(far)
    return swap_cores(near), far


def partner(value, mask):
    return lax.ppermute(value, "space", [(i, i ^ mask) for i in range(lax.axis_size("space"))])


def pairs_of_groups(block, first):
    count = lax.axis_size("depth")
    pairs = [(i, i + 1) for i in range(first, count - 1, 2)]
    return lax.ppermute(block, "depth", pairs + [(b, a) for a, b in pairs])


def body(c_points, adjoint_points, conv1_weight, conv2_weight, bias1):
    _, chans, height, breadth = c_points.shape
    layers = conv1_weight.shape[0]
    tiles = lax.axis_size("space")
    scale = 1.0 / math.sqrt(height * tiles * breadth)
    pix = height * breadth
    wide = 3 * chans
    S = jax.ShapeDtypeStruct
    tile32, tile16 = S((chans, pix), F32), S((chans, pix), BF16)
    rows16 = lambda rows: S((chans, rows * breadth), BF16)
    stack = lambda rows: S((wide, rows * breadth), BF16)
    row_flops = 2 * wide * wide * breadth

    s0, s0h = call(entry_kernel, [tile32, tile16], [c_points])
    near1 = swap_cores(s0h)
    q4, b3 = call(adjoint_kernel, [tile32, tile16], [adjoint_points])
    far1 = swap_chips(call(pack_kernel, [rows16(10)], [s0h, near1, b3])[0])
    mats = S((layers, 2, wide, wide), BF16)
    fw, bias = call(prepare_kernel, [mats, S((128, 8), F32)], [conv1_weight, conv2_weight, bias1])
    bw = call(turn_kernel, [mats], [conv1_weight, conv2_weight])[0]
    far1, fw, bias, bw = lax.optimization_barrier((far1, fw, bias, bw))
    near2 = swap_cores(call(pass_kernel, [rows16(6)], [far1, b3])[0])
    f16, x0, x1, x2, x3, a0, a1, a2, a3 = call(
        forward_kernel,
        [tile16, *[stack(6)] * 4, stack(6), stack(6), stack(10), stack(6)],
        [s0, near1, far1, near2, fw, bias],
        [VMEM((wide, 20 * breadth), BF16), VMEM((wide, 18 * breadth), BF16), VMEM((chans, 16 * breadth), F32)],
        flops=104 * row_flops,
    )

    def single(pos, skip, base, adjoint, core, chip, hidden, final):
        outs = [tile32, tile16] if final is None else [tile16] * 3
        args = [adjoint, core, chip, hidden, bw]

        def kernel(*refs):
            given, refs = refs[: len(args)], refs[len(args) :]
            held = None if final is None else given[5]
            results, rest = refs[: len(outs)], refs[len(outs) :]
            single_kernel(pos, skip, base, *given[:5], held, results, *rest)

        if final is not None:
            args.append(final)
        return call(
            kernel,
            [*outs, tile16],
            args,
            [VMEM((wide, 8 * breadth), BF16), VMEM((wide, 6 * breadth), BF16)],
            flops=14 * row_flops,
        )

    def grads(skip, b, hidden, e, inputs):
        return call(
            functools.partial(grad_kernel, skip),
            [S((2, CHUNK, 128), F32)],
            [b, hidden, e, inputs],
            [VMEM((wide, 6 * breadth), BF16)] * 2,
            flops=12 * row_flops,
        )[0]

    q3, b2h, e3 = single(3, 0, (4, 8), q4, near2, far1, a3, None)
    near3, far3 = swaps(b2h, b2h)
    g3 = grads(0, b3, a3, e3, x3)
    q1, near4, far4, b2, e2, b1, e1 = call(
        functools.partial(double_kernel, 2),
        [tile32, rows16(2), rows16(2), tile16, tile16, tile16, tile16],
        [q3, near3, far3, a2, a1, bw],
        [VMEM((wide, 12 * breadth), BF16), VMEM((wide, 10 * breadth), BF16), VMEM((chans, 8 * breadth), F32)],
        flops=36 * row_flops,
    )
    near4, far4, g3 = lax.optimization_barrier((near4, far4, g3))
    near4, far4 = swaps(near4, far4)
    g2 = grads(2, b2, a2, e2, x2)
    g1 = grads(0, b1, a1, e1, x1)
    pair, far, b0, e0 = single(0, 0, (0, 0), q1, near4, far4, a0, f16)
    g0 = grads(0, b0, a0, e0, x0)

    def chunks(n, kind):
        return S((n, CHUNK, 128), kind)

    send, keep = call(split_kernel, [chunks(4, BF16), chunks(4, F32)], [g0, g1, g2, g3])
    keep, *sends = call(spread_kernel, [chunks(1, F32)] + [chunks(1, BF16)] * 3, [keep, partner(send, 1)])
    parts = [partner(value, 2 * (k + 1)) for k, value in enumerate(sends)]
    far = pairs_of_groups(far, 1)
    pair = pairs_of_groups(pair, 0)
    mine = call(total_kernel, [chunks(1, BF16)], [keep, *parts])[0]
    parts = [partner(mine, 8 * (k + 1)) for k in range(3)]
    mine = call(total_kernel, [chunks(1, BF16)], [mine, *parts])[0]
    mine, pair, far = lax.optimization_barrier((mine, pair, far))
    parts = [partner(mine, 2 * (k + 1)) for k in range(3)]
    points, adjoints = call(
        points_kernel, [S(c_points.shape, F32), S(c_points.shape, F32)], [c_points, adjoint_points, pair, far]
    )
    mine = call(join_kernel, [chunks(4, BF16)], [mine, *parts])[0]
    mine, points, adjoints = lax.optimization_barrier((mine, points, adjoints))
    part = partner(mine, 1)
    one, two, vec = exit_calls(scale, mine, part, S(conv1_weight.shape, F32), S(bias1.shape, F32))
    return points, adjoints, one, two, vec


def solution(mesh):
    in_specs = (
        P("depth", None, "space", None),
        P("depth", None, "space", None),
        P("depth", None, None),
        P("depth", None, None),
        P("depth", None),
    )
    out_specs = in_specs[:2] + (P("depth", None, None), P("depth", None, None), P("depth", None))

    def run(*args):
        return tuple(body(*args))

    return jax.shard_map(run, mesh=mesh, in_specs=in_specs, out_specs=out_specs, check_vma=False)
```

```python
import functools
import math

import jax
import jax.numpy as jnp
from jax import lax
from jax.experimental import pallas as pl
from jax.experimental.pallas import tpu as pltpu
from jax.sharding import PartitionSpec as P


STEP = 0.25
F32 = jnp.float32
BF16 = jnp.bfloat16
VMEM = pltpu.VMEM


def lanes(j, breadth, rows=1):
    return slice(j * breadth, (j + rows) * breadth)


def put_stack(dst, j, row):
    chans, breadth = row.shape
    row = row.astype(BF16)
    col = lax.broadcasted_iota(jnp.int32, row.shape, 1)
    none = jnp.zeros((), BF16)
    left = jnp.where(col == 0, none, pltpu.roll(row, 1, axis=1))
    right = jnp.where(col == breadth - 1, none, pltpu.roll(row, breadth - 1, axis=1))
    dst[0:chans, lanes(j, breadth)] = left
    dst[chans : 2 * chans, lanes(j, breadth)] = row
    dst[2 * chans : 3 * chans, lanes(j, breadth)] = right


def conv(src, first, rows, weight, chans, breadth):
    one = two = None
    for j in range(0, rows + 2, 2):
        both = jnp.dot(weight, src[:, lanes(first + j, breadth, 2)], preferred_element_type=F32)
        for half in range(2):
            z = both[:, lanes(half, breadth)]
            k = j + half - 2
            if k >= 0:
                yield k, two + z[2 * chans :]
            two = one + z[chans : 2 * chans] if one is not None else None
            one = z[:chans]


def even_tile():
    return lax.axis_index("space") % 2 == 0


def halo_rows(core, chip, even, breadth, row, depth=4, base=(0, 0)):
    at = row + depth if row < 0 else row - 4
    near = core[:, lanes(base[0] + at, breadth)]
    far = chip[:, lanes(base[1] + at, breadth)]
    return (jnp.where(even, far, near) if row < 0 else jnp.where(even, near, far)).astype(F32)


def wide_rows(own, core, chip, edge, even, breadth, row):
    if 0 <= row < 4:
        return own[:, lanes(row, breadth)]
    at = row + 8 if row < 0 else row - 4
    far = chip[:, lanes(at, breadth)]
    if row < 0:
        near = edge[:, lanes(at, breadth)] if at < 4 else core[:, lanes(at - 4, breadth)]
        return jnp.where(even, far, near).astype(F32)
    near = core[:, lanes(at, breadth)] if at < 4 else edge[:, lanes(at - 4, breadth)]
    return jnp.where(even, near, far).astype(F32)


def put_edge(dst, base, for_above, rows, breadth):
    for k in range(2):
        value = jnp.where(for_above, rows[k + 2].astype(BF16), rows[k].astype(BF16))
        dst[:, lanes(base + k, breadth)] = value


def gate(value, row):
    index = lax.axis_index("space")
    if row < 0:
        return jnp.where(index >= (3 - row) // 4, value, 0.0)
    if row >= 4:
        return jnp.where(index + row // 4 < lax.axis_size("space"), value, 0.0)
    return value


def softplus(value):
    return jnp.maximum(value, 0.0) + jnp.log1p(jnp.exp(-jnp.abs(value)))


def entry_kernel(field, flat, flat16):
    _, _, height, breadth = field.shape
    for r in range(height):
        at = lanes(r, breadth)
        value = field[0, :, r, :]
        flat[:, at] = value
        flat16[:, at] = value.astype(BF16)


def adjoint_kernel(q, q4, b3):
    _, _, height, breadth = q.shape
    for r in range(height):
        at = lanes(r, breadth)
        value = q[0, :, r, :]
        q4[:, at] = value
        b3[:, at] = (STEP * value).astype(BF16)


def pack_kernel(own, core, b, out):
    even = even_tile()
    breadth = own.shape[1] // 4
    out[:, lanes(0, breadth, 4)] = jnp.where(even, own[...], core[...])
    out[:, lanes(4, breadth, 4)] = jnp.where(even, core[...], own[...])
    put_edge(out, 8, jnp.logical_not(even), [b[:, lanes(k, breadth)] for k in range(4)], breadth)


def pass_kernel(chip, b, out):
    even = even_tile()
    breadth = b.shape[1] // 4
    out[:, lanes(0, breadth, 4)] = jnp.where(even, chip[:, lanes(4, breadth, 4)], chip[:, lanes(0, breadth, 4)])
    put_edge(out, 4, even, [b[:, lanes(k, breadth)] for k in range(4)], breadth)


def prepare_kernel(w1, w2, bias, forward, columns):
    layers, chans, _ = w1.shape
    wide = 3 * chans
    for l in range(layers):
        for which, w in enumerate((w1, w2)):
            for dy in range(3):
                forward[l, which, dy * chans : (dy + 1) * chans, :] = w[l, :, dy * wide : (dy + 1) * wide]
    rows = jnp.concatenate([bias[...], jnp.zeros((8 - layers, chans), F32)], axis=0)
    columns[...] = jnp.concatenate([rows, jnp.zeros((8, 128 - chans), F32)], axis=1).T


def turn_kernel(w1, w2, backward):
    layers, chans, _ = w1.shape
    for l in range(layers):
        for which, w in enumerate((w1, w2)):
            turned = w[l].astype(F32).T
            for e in range(3):
                blocks = [turned[(8 - 3 * e - s) * chans : (9 - 3 * e - s) * chans] for s in range(3)]
                backward[l, which, e * chans : (e + 1) * chans, :] = jnp.concatenate(blocks, axis=1).astype(BF16)


def forward_kernel(state, core, chip, edge, weights, bias, out, *refs):
    inputs, hidden, (xs, wide_a, mid) = refs[0:4], refs[4:8], refs[8:]
    chans, breadth = state.shape[0], state.shape[1] // 4
    even = even_tile()
    start = functools.partial(wide_rows, state, core, chip, edge, even, breadth)
    for row in range(-8, 12):
        put_stack(xs, row + 8, start(row))
    for pos in range(4):
        reach = 8 - 2 * pos
        inputs[pos][...] = xs[:, lanes(reach - 1, breadth, 6)]
        offset = bias[0:chans, pos : pos + 1]
        dst = wide_a if pos < 2 else hidden[pos]
        for k, value in conv(xs, 0, 2 + 2 * reach, weights[pos, 0], chans, breadth):
            put_stack(dst, k, gate(softplus(value + offset), k + 1 - reach))
        if pos < 2:
            hidden[pos][...] = dst[:, lanes(reach - 2, breadth, 6)]
        if pos == 3:
            break
        for k, value in conv(dst, 0, 2 * reach, weights[pos, 1], chans, breadth):
            row = k + 2 - reach
            at = lanes(row + 6, breadth)
            value = gate((mid[:, at] if pos else start(row)) + STEP * value, row)
            put_stack(xs, k, value)
            mid[:, at] = value
            if pos == 2 and 0 <= row < 4:
                out[:, lanes(row, breadth)] = value


def last_kernel(state, hidden, weights, out):
    chans, breadth = state.shape[0], state.shape[1] // 4
    for k, value in conv(hidden, 0, 4, weights[3, 1], chans, breadth):
        at = lanes(k, breadth)
        out[:, at] = (state[:, at] + STEP * value).astype(BF16)


def slope(stack, j, chans, breadth):
    return 1.0 - jnp.exp(-stack[chans : 2 * chans, lanes(j, breadth)].astype(F32))


def single_kernel(pos, skip, base, adjoint, core, chip, hidden, weights, final, outs, e16, bs, es):
    chans, breadth = adjoint.shape[0], adjoint.shape[1] // 4
    even = even_tile()
    for row in range(-2, 6):
        if 0 <= row < 4:
            value = STEP * adjoint[:, lanes(row, breadth)]
        else:
            value = halo_rows(core, chip, even, breadth, row, 2, base)
        put_stack(bs, row + 2, value)
    for k, value in conv(bs, 0, 6, weights[pos, 1], chans, breadth):
        row = k - 1
        value = gate(value * slope(hidden, k + skip, chans, breadth), row)
        if 0 <= row < 4:
            e16[:, lanes(row, breadth)] = value.astype(BF16)
        put_stack(es, k, value)
    for k, value in conv(es, 0, 4, weights[pos, 0], chans, breadth):
        at = lanes(k, breadth)
        value = adjoint[:, at] + value
        if final is None:
            outs[0][:, at] = value
            outs[1][:, at] = (STEP * value).astype(BF16)
        else:
            value = value.astype(BF16)
            outs[0][:, at] = jnp.where(even_group(), final[:, at], value)
            outs[1][:, at] = jnp.where(even_group(), value, final[:, at])


def even_group():
    return lax.axis_index("depth") % 2 == 0


def double_kernel(pos, adjoint, core, chip, ha, hb, weights, out, near, far, bc16, ba16, ea16, bb16, eb16, bs, es, mid):
    chans, breadth = adjoint.shape[0], adjoint.shape[1] // 4
    even = even_tile()
    for row in range(-4, 8):
        if 0 <= row < 4:
            value = STEP * adjoint[:, lanes(row, breadth)]
            ba16[:, lanes(row, breadth)] = value.astype(BF16)
        else:
            value = halo_rows(core, chip, even, breadth, row)
        put_stack(bs, row + 4, value)
    for k, value in conv(bs, 0, 10, weights[pos, 1], chans, breadth):
        row = k - 3
        value = gate(value * slope(ha, k, chans, breadth), row)
        if 0 <= row < 4:
            ea16[:, lanes(row, breadth)] = value.astype(BF16)
        put_stack(es, k, value)
    for k, value in conv(es, 0, 8, weights[pos, 0], chans, breadth):
        row = k - 2
        if 0 <= row < 4:
            value = adjoint[:, lanes(row, breadth)] + value
        else:
            value = 4.0 * halo_rows(core, chip, even, breadth, row) + value
        value = gate(value, row)
        mid[:, lanes(k, breadth)] = value
        value = STEP * value
        if 0 <= row < 4:
            bb16[:, lanes(row, breadth)] = value.astype(BF16)
        put_stack(bs, k, value)
    for k, value in conv(bs, 0, 6, weights[pos - 1, 1], chans, breadth):
        row = k - 1
        value = gate(value * slope(hb, k, chans, breadth), row)
        if 0 <= row < 4:
            eb16[:, lanes(row, breadth)] = value.astype(BF16)
        put_stack(es, k, value)
    rows = []
    for k, value in conv(es, 0, 4, weights[pos - 1, 0], chans, breadth):
        value = mid[:, lanes(k + 2, breadth)] + value
        out[:, lanes(k, breadth)] = value
        rows.append(STEP * value)
        bc16[:, lanes(k, breadth)] = rows[k].astype(BF16)
    put_edge(near, 0, even, rows, breadth)
    put_edge(far, 0, jnp.logical_not(even), rows, breadth)


def outer(left, right):
    return lax.dot_general(left, right, (((1,), (1,)), ((), ())), preferred_element_type=F32)


CHUNK = 4 * 72 + 8


def taps(src, dst):
    chans, breadth = src.shape[0], src.shape[1] // 4
    dst[...] = jnp.zeros_like(dst)
    for dy in range(3):
        dst[dy * chans : (dy + 1) * chans, lanes(dy, breadth, 4)] = src[...]


def two_kernel(b, hidden, out, bd):
    taps(b, bd)
    out[...] = outer(bd[...], hidden[...])


def put_grads(two, e, inputs, pay, ed):
    chans = e.shape[0]
    taps(e, ed)
    both = jnp.concatenate([two, outer(ed[...], inputs[...])], axis=1)
    for c in range(8):
        for t in range(3):
            at = 72 * (c % 4) + 24 * t
            pay[c // 4, at : at + 24, :] = both[24 * c : 24 * c + 24, 128 * t : 128 * t + 128]
    for c in range(2):
        pay[c, 288:CHUNK, :] = jnp.zeros((8, 128), F32)
    ones = jnp.ones((8, e.shape[1]), BF16)
    pay[0, 288:289, 0:chans] = outer(ones, e[...])[0:1]


def one_kernel(two, e, inputs, pay, ed):
    put_grads(two[...], e, inputs, pay, ed)


def grad_kernel(skip, b, hidden, e, inputs, pay, bd, ed):
    taps(b, bd)
    two = outer(bd[...], hidden[:, lanes(skip, b.shape[1] // 4, 6)])
    put_grads(two, e, inputs, pay, ed)


def put_packed(dst, at, total):
    tail = total[288:CHUNK]
    bias = tail[0:1] + tail[1:2]
    head = bias.astype(BF16).astype(F32)
    row = lax.broadcasted_iota(jnp.int32, tail.shape, 0)
    tail = jnp.where(row == 0, head, jnp.where(row == 1, bias - head, 0.0))
    dst[at, 0:288] = total[0:288].astype(BF16)
    dst[at, 288:CHUNK] = tail.astype(BF16)


def where_am_i():
    index = lax.axis_index("space")
    return index % 2, (index // 2) % 4, index // 8


def split_kernel(g0, g1, g2, g3, send, keep):
    core, _, _ = where_am_i()
    for k in range(2):
        for at, low, high in ((k, g0, g2), (k + 2, g1, g3)):
            a, b = low[k], high[k]
            keep[at] = jnp.where(core == 0, a, b)
            put_packed(send, at, jnp.where(core == 0, b, a))


def spread_kernel(keep_in, part, keep, *sends):
    _, mine, _ = where_am_i()
    for k, dst in enumerate((keep, *sends)):
        total = keep_in[mine ^ k] + part[mine ^ k].astype(F32)
        if k == 0:
            dst[0] = total
        else:
            put_packed(dst, 0, total)


def total_kernel(own, part1, part2, part3, out):
    pairs = own[0].astype(F32) + part1[0].astype(F32), part2[0].astype(F32) + part3[0].astype(F32)
    put_packed(out, 0, pairs[0] + pairs[1])


def join_kernel(own, part1, part2, part3, out):
    _, mine, _ = where_am_i()
    for k, src in enumerate((own, part1, part2, part3)):
        out[mine ^ k] = src[0]


def points_kernel(c, q, pair, far, points, adjoints):
    _, _, height, breadth = c.shape
    group = lax.axis_index("depth")
    first, last = group == 0, group == lax.axis_size("depth") - 1
    for r in range(height):
        at = lanes(r, breadth)
        a, b = pair[:, at].astype(F32), far[:, at].astype(F32)
        points[0, :, r, :] = jnp.where(first, c[0, :, r, :], jnp.where(even_group(), b, a))
        adjoints[0, :, r, :] = jnp.where(last, q[0, :, r, :], jnp.where(even_group(), a, b))


def lay_out(scale, src, base, one, two, wide_one, wide_two, sems):
    chans = wide_one.shape[1]
    wide = 3 * chans
    copies = []
    for l in range(2):
        cols = []
        for t in range(3):
            at = [(2 * l + k // 4, 72 * (k % 4) + 24 * t) for k in range(8)]
            cols.append(jnp.concatenate([src[c, r : r + 24, :].astype(F32) for c, r in at], axis=0))
        full = jnp.concatenate(cols, axis=1) * scale
        for dy in range(3):
            rows = full[dy * chans : (dy + 1) * chans]
            wide_two[l, :, dy * wide : (dy + 1) * wide] = rows[:, :wide]
            wide_one[l, :, dy * wide : (dy + 1) * wide] = rows[:, wide:]
        for k, (held, out) in enumerate(((wide_one, one), (wide_two, two))):
            copy = pltpu.make_async_copy(held.at[l], out.at[base + l], sems.at[2 * l + k])
            copy.start()
            copies.append(copy)
    return copies


def exit_own_kernel(scale, own, one, two, wide_one, wide_two, sems):
    core, _, _ = where_am_i()
    for copy in lay_out(scale, own, 2 * core, one, two, wide_one, wide_two, sems):
        copy.wait()


def exit_other_kernel(scale, part, own, _one, _two, one, two, bias, wide_one, wide_two, sems, vec, sem):
    core, _, _ = where_am_i()
    chans = vec.shape[1]
    for l in range(vec.shape[0]):
        at = (2 * (l % 2), slice(288, 290), slice(0, chans))
        low = jnp.where(core == l // 2, own[at].astype(F32), part[at].astype(F32))
        vec[l : l + 1, :] = (low[0:1] + low[1:2]) * scale
    last = pltpu.make_async_copy(vec, bias, sem)
    last.start()
    for copy in lay_out(scale, part, 2 * (1 - core), one, two, wide_one, wide_two, sems):
        copy.wait()
    last.wait()


def exit_calls(scale, mine, part, grad, vec):
    _, chans, wide = grad.shape
    hbm = pl.BlockSpec(memory_space=pl.ANY)
    near = pl.BlockSpec(memory_space=VMEM)
    scratch = [VMEM((2, chans, wide), F32)] * 2 + [pltpu.SemaphoreType.DMA((4,))]
    options = dict(
        cost_estimate=pl.CostEstimate(flops=0, bytes_accessed=16 * chans * wide, transcendentals=0),
        compiler_params=pltpu.CompilerParams(vmem_limit_bytes=40 << 20),
    )
    held = pl.pallas_call(
        functools.partial(exit_own_kernel, scale),
        out_shape=[grad, grad],
        in_specs=[near],
        out_specs=[hbm, hbm],
        scratch_shapes=scratch,
        name="exit_own",
        **options,
    )(mine)
    return pl.pallas_call(
        functools.partial(exit_other_kernel, scale),
        out_shape=[grad, grad, vec],
        in_specs=[near, near, hbm, hbm],
        out_specs=[hbm, hbm, hbm],
        scratch_shapes=[*scratch, VMEM(vec.shape, F32), pltpu.SemaphoreType.DMA],
        input_output_aliases={2: 0, 3: 1},
        name="exit_other",
        **options,
    )(part, mine, *held)


def call(kernel, outs, args, scratch=(), flops=0):
    size = sum(math.prod(a.shape) * a.dtype.itemsize for a in (*args, *outs))
    return pl.pallas_call(
        kernel,
        out_shape=outs,
        in_specs=[pl.BlockSpec(memory_space=VMEM) for _ in args],
        out_specs=[pl.BlockSpec(memory_space=VMEM) for _ in outs],
        scratch_shapes=list(scratch),
        cost_estimate=pl.CostEstimate(flops=flops, bytes_accessed=size, transcendentals=0),
        compiler_params=pltpu.CompilerParams(vmem_limit_bytes=40 << 20),
    )(*args)


def swap_cores(value):
    return lax.ppermute(value, "space", [(i, i ^ 1) for i in range(lax.axis_size("space"))])


def swap_chips(value):
    count = lax.axis_size("space")
    return lax.ppermute(value, "space", [(i, i + 1 if i % 2 else i - 1) for i in range(1, count - 1)])


def swaps(near, far):
    far = swap_chips(far)
    return swap_cores(near), far


def partner(value, mask):
    return lax.ppermute(value, "space", [(i, i ^ mask) for i in range(lax.axis_size("space"))])


def pairs_of_groups(block, first):
    count = lax.axis_size("depth")
    pairs = [(i, i + 1) for i in range(first, count - 1, 2)]
    return lax.ppermute(block, "depth", pairs + [(b, a) for a, b in pairs])


def body(c_points, adjoint_points, conv1_weight, conv2_weight, bias1):
    _, chans, height, breadth = c_points.shape
    layers = conv1_weight.shape[0]
    tiles = lax.axis_size("space")
    scale = 1.0 / math.sqrt(height * tiles * breadth)
    pix = height * breadth
    wide = 3 * chans
    S = jax.ShapeDtypeStruct
    tile32, tile16 = S((chans, pix), F32), S((chans, pix), BF16)
    rows16 = lambda rows: S((chans, rows * breadth), BF16)
    stack = lambda rows: S((wide, rows * breadth), BF16)
    row_flops = 2 * wide * wide * breadth

    s0, s0h = call(entry_kernel, [tile32, tile16], [c_points])
    near1 = swap_cores(s0h)
    q4, b3 = call(adjoint_kernel, [tile32, tile16], [adjoint_points])
    far1 = swap_chips(call(pack_kernel, [rows16(10)], [s0h, near1, b3])[0])
    mats = S((layers, 2, wide, wide), BF16)
    fw, bias = call(prepare_kernel, [mats, S((128, 8), F32)], [conv1_weight, conv2_weight, bias1])
    bw = call(turn_kernel, [mats], [conv1_weight, conv2_weight])[0]
    far1, fw, bias, bw = lax.optimization_barrier((far1, fw, bias, bw))
    near2 = swap_cores(call(pass_kernel, [rows16(6)], [far1, b3])[0])
    s3, x0, x1, x2, x3, a0, a1, a2, a3 = call(
        forward_kernel,
        [tile32, *[stack(6)] * 4, stack(6), stack(6), stack(10), stack(6)],
        [s0, near1, far1, near2, fw, bias],
        [VMEM((wide, 20 * breadth), BF16), VMEM((wide, 18 * breadth), BF16), VMEM((chans, 16 * breadth), F32)],
        flops=98 * row_flops,
    )
    f16 = call(last_kernel, [tile16], [s3, a3, fw], flops=6 * row_flops)[0]

    def single(pos, skip, base, adjoint, core, chip, hidden, final):
        outs = [tile32, tile16] if final is None else [tile16] * 2
        args = [adjoint, core, chip, hidden, bw]

        def kernel(*refs):
            given, refs = refs[: len(args)], refs[len(args) :]
            held = None if final is None else given[5]
            results, rest = refs[: len(outs)], refs[len(outs) :]
            single_kernel(pos, skip, base, *given[:5], held, results, *rest)

        if final is not None:
            args.append(final)
        return call(
            kernel,
            [*outs, tile16],
            args,
            [VMEM((wide, 8 * breadth), BF16), VMEM((wide, 6 * breadth), BF16)],
            flops=14 * row_flops,
        )

    def grads(skip, b, hidden, e, inputs):
        return call(
            functools.partial(grad_kernel, skip),
            [S((2, CHUNK, 128), F32)],
            [b, hidden, e, inputs],
            [VMEM((wide, 6 * breadth), BF16)] * 2,
            flops=12 * row_flops,
        )[0]

    q3, b2h, e3 = single(3, 0, (4, 8), q4, near2, far1, a3, None)
    near3, far3 = swaps(b2h, b2h)
    g3 = grads(0, b3, a3, e3, x3)
    q1, near4, far4, b0, b2, e2, b1, e1 = call(
        functools.partial(double_kernel, 2),
        [tile32, rows16(2), rows16(2), *[tile16] * 5],
        [q3, near3, far3, a2, a1, bw],
        [VMEM((wide, 12 * breadth), BF16), VMEM((wide, 10 * breadth), BF16), VMEM((chans, 8 * breadth), F32)],
        flops=36 * row_flops,
    )
    near4, far4, g3, f16 = lax.optimization_barrier((near4, far4, g3, f16))
    near4, far4 = swaps(near4, far4)
    g2 = grads(2, b2, a2, e2, x2)
    g1 = grads(0, b1, a1, e1, x1)
    square = S((wide, wide), F32)
    taps_scratch = [VMEM((wide, 6 * breadth), BF16)]
    two0 = call(two_kernel, [square], [b0, a0], taps_scratch, flops=6 * row_flops)[0]
    pair, far, e0 = single(0, 0, (0, 0), q1, near4, far4, a0, f16)
    g0 = call(one_kernel, [S((2, CHUNK, 128), F32)], [two0, e0, x0], taps_scratch, flops=6 * row_flops)[0]

    def chunks(n, kind):
        return S((n, CHUNK, 128), kind)

    send, keep = call(split_kernel, [chunks(4, BF16), chunks(4, F32)], [g0, g1, g2, g3])
    keep, *sends = call(spread_kernel, [chunks(1, F32)] + [chunks(1, BF16)] * 3, [keep, partner(send, 1)])
    parts = [partner(value, 2 * (k + 1)) for k, value in enumerate(sends)]
    far = pairs_of_groups(far, 1)
    pair = pairs_of_groups(pair, 0)
    mine = call(total_kernel, [chunks(1, BF16)], [keep, *parts])[0]
    parts = [partner(mine, 8 * (k + 1)) for k in range(3)]
    mine = call(total_kernel, [chunks(1, BF16)], [mine, *parts])[0]
    mine, pair, far = lax.optimization_barrier((mine, pair, far))
    parts = [partner(mine, 2 * (k + 1)) for k in range(3)]
    points, adjoints = call(
        points_kernel, [S(c_points.shape, F32), S(c_points.shape, F32)], [c_points, adjoint_points, pair, far]
    )
    mine = call(join_kernel, [chunks(4, BF16)], [mine, *parts])[0]
    mine, points, adjoints = lax.optimization_barrier((mine, points, adjoints))
    part = partner(mine, 1)
    one, two, vec = exit_calls(scale, mine, part, S(conv1_weight.shape, F32), S(bias1.shape, F32))
    return points, adjoints, one, two, vec


def solution(mesh):
    in_specs = (
        P("depth", None, "space", None),
        P("depth", None, "space", None),
        P("depth", None, None),
        P("depth", None, None),
        P("depth", None),
    )
    out_specs = in_specs[:2] + (P("depth", None, None), P("depth", None, None), P("depth", None))

    def run(*args):
        return tuple(body(*args))

    return jax.shard_map(run, mesh=mesh, in_specs=in_specs, out_specs=out_specs, check_vma=False)
```

```python
import functools
import math

import jax
import jax.numpy as jnp
from jax import lax
from jax.experimental import pallas as pl
from jax.experimental.pallas import tpu as pltpu
from jax.sharding import PartitionSpec as P


STEP = 0.25
F32 = jnp.float32
BF16 = jnp.bfloat16
VMEM = pltpu.VMEM


def lanes(j, breadth, rows=1):
    return slice(j * breadth, (j + rows) * breadth)


def put_stack(dst, j, row):
    chans, breadth = row.shape
    row = row.astype(BF16)
    col = lax.broadcasted_iota(jnp.int32, row.shape, 1)
    none = jnp.zeros((), BF16)
    left = jnp.where(col == 0, none, pltpu.roll(row, 1, axis=1))
    right = jnp.where(col == breadth - 1, none, pltpu.roll(row, breadth - 1, axis=1))
    dst[0:chans, lanes(j, breadth)] = left
    dst[chans : 2 * chans, lanes(j, breadth)] = row
    dst[2 * chans : 3 * chans, lanes(j, breadth)] = right


def conv(src, first, rows, weight, chans, breadth):
    one = two = None
    for j in range(0, rows + 2, 2):
        both = jnp.dot(weight, src[:, lanes(first + j, breadth, 2)], preferred_element_type=F32)
        for half in range(2):
            z = both[:, lanes(half, breadth)]
            k = j + half - 2
            if k >= 0:
                yield k, two + z[2 * chans :]
            two = one + z[chans : 2 * chans] if one is not None else None
            one = z[:chans]


def even_tile():
    return lax.axis_index("space") % 2 == 0


def halo_rows(core, chip, even, breadth, row, depth=4, base=(0, 0)):
    at = row + depth if row < 0 else row - 4
    near = core[:, lanes(base[0] + at, breadth)]
    far = chip[:, lanes(base[1] + at, breadth)]
    return (jnp.where(even, far, near) if row < 0 else jnp.where(even, near, far)).astype(F32)


def wide_rows(own, core, chip, edge, even, breadth, row):
    if 0 <= row < 4:
        return own[:, lanes(row, breadth)]
    at = row + 8 if row < 0 else row - 4
    far = chip[:, lanes(at, breadth)]
    if row < 0:
        near = edge[:, lanes(at, breadth)] if at < 4 else core[:, lanes(at - 4, breadth)]
        return jnp.where(even, far, near).astype(F32)
    near = core[:, lanes(at, breadth)] if at < 4 else edge[:, lanes(at - 4, breadth)]
    return jnp.where(even, near, far).astype(F32)


def put_edge(dst, base, for_above, rows, breadth):
    for k in range(2):
        value = jnp.where(for_above, rows[k + 2].astype(BF16), rows[k].astype(BF16))
        dst[:, lanes(base + k, breadth)] = value


def gate(value, row):
    index = lax.axis_index("space")
    if row < 0:
        return jnp.where(index >= (3 - row) // 4, value, 0.0)
    if row >= 4:
        return jnp.where(index + row // 4 < lax.axis_size("space"), value, 0.0)
    return value


def softplus(value):
    return jnp.maximum(value, 0.0) + jnp.log1p(jnp.exp(-jnp.abs(value)))


def entry_kernel(field, flat, flat16):
    _, _, height, breadth = field.shape
    for r in range(height):
        at = lanes(r, breadth)
        value = field[0, :, r, :]
        flat[:, at] = value
        flat16[:, at] = value.astype(BF16)


def adjoint_kernel(q, q4, b3):
    _, _, height, breadth = q.shape
    for r in range(height):
        at = lanes(r, breadth)
        value = q[0, :, r, :]
        q4[:, at] = value
        b3[:, at] = (STEP * value).astype(BF16)


def pack_kernel(own, core, b, out):
    even = even_tile()
    breadth = own.shape[1] // 4
    out[:, lanes(0, breadth, 4)] = jnp.where(even, own[...], core[...])
    out[:, lanes(4, breadth, 4)] = jnp.where(even, core[...], own[...])
    put_edge(out, 8, jnp.logical_not(even), [b[:, lanes(k, breadth)] for k in range(4)], breadth)


def pass_kernel(chip, b, out):
    even = even_tile()
    breadth = b.shape[1] // 4
    out[:, lanes(0, breadth, 4)] = jnp.where(even, chip[:, lanes(4, breadth, 4)], chip[:, lanes(0, breadth, 4)])
    put_edge(out, 4, even, [b[:, lanes(k, breadth)] for k in range(4)], breadth)


def prepare_kernel(w1, w2, bias, forward, columns):
    layers, chans, _ = w1.shape
    wide = 3 * chans
    for l in range(layers):
        for which, w in enumerate((w1, w2)):
            for dy in range(3):
                forward[l, which, dy * chans : (dy + 1) * chans, :] = w[l, :, dy * wide : (dy + 1) * wide]
    rows = jnp.concatenate([bias[...], jnp.zeros((8 - layers, chans), F32)], axis=0)
    columns[...] = jnp.concatenate([rows, jnp.zeros((8, 128 - chans), F32)], axis=1).T


def turn_kernel(w1, w2, backward):
    layers, chans, _ = w1.shape
    for l in range(layers):
        for which, w in enumerate((w1, w2)):
            turned = w[l].astype(F32).T
            for e in range(3):
                blocks = [turned[(8 - 3 * e - s) * chans : (9 - 3 * e - s) * chans] for s in range(3)]
                backward[l, which, e * chans : (e + 1) * chans, :] = jnp.concatenate(blocks, axis=1).astype(BF16)


def forward_kernel(state, core, chip, edge, weights, bias, out, *refs):
    inputs, hidden, (xs, wide_a, mid) = refs[0:4], refs[4:8], refs[8:]
    chans, breadth = state.shape[0], state.shape[1] // 4
    even = even_tile()
    start = functools.partial(wide_rows, state, core, chip, edge, even, breadth)
    for row in range(-8, 12):
        put_stack(xs, row + 8, start(row))
    for pos in range(4):
        reach = 8 - 2 * pos
        inputs[pos][...] = xs[:, lanes(reach - 1, breadth, 6)]
        offset = bias[0:chans, pos : pos + 1]
        dst = wide_a if pos < 2 else hidden[pos]
        for k, value in conv(xs, 0, 2 + 2 * reach, weights[pos, 0], chans, breadth):
            put_stack(dst, k, gate(softplus(value + offset), k + 1 - reach))
        if pos < 2:
            hidden[pos][...] = dst[:, lanes(reach - 2, breadth, 6)]
        if pos == 3:
            break
        for k, value in conv(dst, 0, 2 * reach, weights[pos, 1], chans, breadth):
            row = k + 2 - reach
            at = lanes(row + 6, breadth)
            value = gate((mid[:, at] if pos else start(row)) + STEP * value, row)
            put_stack(xs, k, value)
            mid[:, at] = value
            if pos == 2 and 0 <= row < 4:
                out[:, lanes(row, breadth)] = value


def last_kernel(state, hidden, weights, out):
    chans, breadth = state.shape[0], state.shape[1] // 4
    for k, value in conv(hidden, 0, 4, weights[3, 1], chans, breadth):
        at = lanes(k, breadth)
        out[:, at] = (state[:, at] + STEP * value).astype(BF16)


def slope(stack, j, chans, breadth):
    return 1.0 - jnp.exp(-stack[chans : 2 * chans, lanes(j, breadth)].astype(F32))


def single_kernel(pos, skip, base, adjoint, core, chip, hidden, weights, final, outs, e16, bs, es):
    chans, breadth = adjoint.shape[0], adjoint.shape[1] // 4
    even = even_tile()
    for row in range(-2, 6):
        if 0 <= row < 4:
            value = STEP * adjoint[:, lanes(row, breadth)]
        else:
            value = halo_rows(core, chip, even, breadth, row, 2, base)
        put_stack(bs, row + 2, value)
    for k, value in conv(bs, 0, 6, weights[pos, 1], chans, breadth):
        row = k - 1
        value = gate(value * slope(hidden, k + skip, chans, breadth), row)
        if 0 <= row < 4:
            e16[:, lanes(row, breadth)] = value.astype(BF16)
        put_stack(es, k, value)
    for k, value in conv(es, 0, 4, weights[pos, 0], chans, breadth):
        at = lanes(k, breadth)
        value = adjoint[:, at] + value
        if final is None:
            outs[0][:, at] = value
            outs[1][:, at] = (STEP * value).astype(BF16)
        else:
            value = value.astype(BF16)
            outs[0][:, at] = jnp.where(even_group(), final[:, at], value)
            outs[1][:, at] = jnp.where(even_group(), value, final[:, at])


def even_group():
    return lax.axis_index("depth") % 2 == 0


def double_kernel(pos, adjoint, core, chip, ha, hb, weights, out, near, far, bc16, ba16, ea16, bb16, eb16, bs, es, mid):
    chans, breadth = adjoint.shape[0], adjoint.shape[1] // 4
    even = even_tile()
    for row in range(-4, 8):
        if 0 <= row < 4:
            value = STEP * adjoint[:, lanes(row, breadth)]
            ba16[:, lanes(row, breadth)] = value.astype(BF16)
        else:
            value = halo_rows(core, chip, even, breadth, row)
        put_stack(bs, row + 4, value)
    for k, value in conv(bs, 0, 10, weights[pos, 1], chans, breadth):
        row = k - 3
        value = gate(value * slope(ha, k, chans, breadth), row)
        if 0 <= row < 4:
            ea16[:, lanes(row, breadth)] = value.astype(BF16)
        put_stack(es, k, value)
    for k, value in conv(es, 0, 8, weights[pos, 0], chans, breadth):
        row = k - 2
        if 0 <= row < 4:
            value = adjoint[:, lanes(row, breadth)] + value
        else:
            value = 4.0 * halo_rows(core, chip, even, breadth, row) + value
        value = gate(value, row)
        mid[:, lanes(k, breadth)] = value
        value = STEP * value
        if 0 <= row < 4:
            bb16[:, lanes(row, breadth)] = value.astype(BF16)
        put_stack(bs, k, value)
    for k, value in conv(bs, 0, 6, weights[pos - 1, 1], chans, breadth):
        row = k - 1
        value = gate(value * slope(hb, k, chans, breadth), row)
        if 0 <= row < 4:
            eb16[:, lanes(row, breadth)] = value.astype(BF16)
        put_stack(es, k, value)
    rows = []
    for k, value in conv(es, 0, 4, weights[pos - 1, 0], chans, breadth):
        value = mid[:, lanes(k + 2, breadth)] + value
        out[:, lanes(k, breadth)] = value
        rows.append(STEP * value)
        bc16[:, lanes(k, breadth)] = rows[k].astype(BF16)
    put_edge(near, 0, even, rows, breadth)
    put_edge(far, 0, jnp.logical_not(even), rows, breadth)


def outer(left, right):
    return lax.dot_general(left, right, (((1,), (1,)), ((), ())), preferred_element_type=F32)


CHUNK = 4 * 72 + 8


def taps(src, dst):
    chans, breadth = src.shape[0], src.shape[1] // 4
    none = jnp.zeros((chans, breadth), dst.dtype)
    for dy in range(3):
        rows = slice(dy * chans, (dy + 1) * chans)
        dst[rows, lanes(dy, breadth, 4)] = src[...]
        for j in (*range(dy), *range(dy + 4, 6)):
            dst[rows, lanes(j, breadth)] = none


def two_kernel(b, hidden, out, bd):
    taps(b, bd)
    out[...] = outer(bd[...], hidden[...])


def put_grads(two, e, inputs, pay, ed):
    chans = e.shape[0]
    taps(e, ed)
    both = jnp.concatenate([two, outer(ed[...], inputs[...])], axis=1)
    for c in range(8):
        for t in range(3):
            at = 72 * (c % 4) + 24 * t
            pay[c // 4, at : at + 24, :] = both[24 * c : 24 * c + 24, 128 * t : 128 * t + 128]
    for c in range(2):
        pay[c, 288:CHUNK, :] = jnp.zeros((8, 128), F32)
    ones = jnp.ones((8, e.shape[1]), BF16)
    pay[0, 288:289, 0:chans] = outer(ones, e[...])[0:1]


def one_kernel(two, e, inputs, pay, ed):
    put_grads(two[...], e, inputs, pay, ed)


def grad_kernel(skip, b, hidden, e, inputs, pay, bd, ed):
    taps(b, bd)
    two = outer(bd[...], hidden[:, lanes(skip, b.shape[1] // 4, 6)])
    put_grads(two, e, inputs, pay, ed)


def put_packed(dst, at, total):
    tail = total[288:CHUNK]
    bias = tail[0:1] + tail[1:2]
    head = bias.astype(BF16).astype(F32)
    row = lax.broadcasted_iota(jnp.int32, tail.shape, 0)
    tail = jnp.where(row == 0, head, jnp.where(row == 1, bias - head, 0.0))
    dst[at, 0:288] = total[0:288].astype(BF16)
    dst[at, 288:CHUNK] = tail.astype(BF16)


def where_am_i():
    index = lax.axis_index("space")
    return index % 2, (index // 2) % 4, index // 8


def split_kernel(g0, g1, g2, g3, send, keep):
    core, _, _ = where_am_i()
    for k in range(2):
        for at, low, high in ((k, g0, g2), (k + 2, g1, g3)):
            a, b = low[k], high[k]
            keep[at] = jnp.where(core == 0, a, b)
            put_packed(send, at, jnp.where(core == 0, b, a))


def spread_kernel(keep_in, part, keep, *sends):
    _, mine, _ = where_am_i()
    for k, dst in enumerate((keep, *sends)):
        total = keep_in[mine ^ k] + part[mine ^ k].astype(F32)
        if k == 0:
            dst[0] = total
        else:
            put_packed(dst, 0, total)


def total_kernel(own, part1, part2, part3, out):
    pairs = own[0].astype(F32) + part1[0].astype(F32), part2[0].astype(F32) + part3[0].astype(F32)
    put_packed(out, 0, pairs[0] + pairs[1])


def join_kernel(own, part1, part2, part3, out):
    _, mine, _ = where_am_i()
    for k, src in enumerate((own, part1, part2, part3)):
        out[mine ^ k] = src[0]


def points_kernel(c, q, pair, far, points, adjoints):
    _, _, height, breadth = c.shape
    group = lax.axis_index("depth")
    first, last = group == 0, group == lax.axis_size("depth") - 1
    for r in range(height):
        at = lanes(r, breadth)
        a, b = pair[:, at].astype(F32), far[:, at].astype(F32)
        points[0, :, r, :] = jnp.where(first, c[0, :, r, :], jnp.where(even_group(), b, a))
        adjoints[0, :, r, :] = jnp.where(last, q[0, :, r, :], jnp.where(even_group(), a, b))


def lay_out(scale, src, base, one, two, wide_one, wide_two, sems):
    chans = wide_one.shape[1]
    wide = 3 * chans
    copies = []
    for l in range(2):
        cols = []
        for t in range(3):
            at = [(2 * l + k // 4, 72 * (k % 4) + 24 * t) for k in range(8)]
            cols.append(jnp.concatenate([src[c, r : r + 24, :].astype(F32) for c, r in at], axis=0))
        full = jnp.concatenate(cols, axis=1) * scale
        for dy in range(3):
            rows = full[dy * chans : (dy + 1) * chans]
            wide_two[l, :, dy * wide : (dy + 1) * wide] = rows[:, :wide]
            wide_one[l, :, dy * wide : (dy + 1) * wide] = rows[:, wide:]
        for k, (held, out) in enumerate(((wide_one, one), (wide_two, two))):
            copy = pltpu.make_async_copy(held.at[l], out.at[base + l], sems.at[2 * l + k])
            copy.start()
            copies.append(copy)
    return copies


def exit_own_kernel(scale, own, one, two, wide_one, wide_two, sems):
    core, _, _ = where_am_i()
    for copy in lay_out(scale, own, 2 * core, one, two, wide_one, wide_two, sems):
        copy.wait()


def exit_other_kernel(scale, part, own, _one, _two, one, two, bias, wide_one, wide_two, sems, vec, sem):
    core, _, _ = where_am_i()
    chans = vec.shape[1]
    for l in range(vec.shape[0]):
        at = (2 * (l % 2), slice(288, 290), slice(0, chans))
        low = jnp.where(core == l // 2, own[at].astype(F32), part[at].astype(F32))
        vec[l : l + 1, :] = (low[0:1] + low[1:2]) * scale
    last = pltpu.make_async_copy(vec, bias, sem)
    last.start()
    for copy in lay_out(scale, part, 2 * (1 - core), one, two, wide_one, wide_two, sems):
        copy.wait()
    last.wait()


def exit_calls(scale, mine, part, grad, vec):
    _, chans, wide = grad.shape
    hbm = pl.BlockSpec(memory_space=pl.ANY)
    near = pl.BlockSpec(memory_space=VMEM)
    scratch = [VMEM((2, chans, wide), F32)] * 2 + [pltpu.SemaphoreType.DMA((4,))]
    options = dict(
        cost_estimate=pl.CostEstimate(flops=0, bytes_accessed=16 * chans * wide, transcendentals=0),
        compiler_params=pltpu.CompilerParams(vmem_limit_bytes=40 << 20),
    )
    held = pl.pallas_call(
        functools.partial(exit_own_kernel, scale),
        out_shape=[grad, grad],
        in_specs=[near],
        out_specs=[hbm, hbm],
        scratch_shapes=scratch,
        name="exit_own",
        **options,
    )(mine)
    return pl.pallas_call(
        functools.partial(exit_other_kernel, scale),
        out_shape=[grad, grad, vec],
        in_specs=[near, near, hbm, hbm],
        out_specs=[hbm, hbm, hbm],
        scratch_shapes=[*scratch, VMEM(vec.shape, F32), pltpu.SemaphoreType.DMA],
        input_output_aliases={2: 0, 3: 1},
        name="exit_other",
        **options,
    )(part, mine, *held)


def call(kernel, outs, args, scratch=(), flops=0):
    size = sum(math.prod(a.shape) * a.dtype.itemsize for a in (*args, *outs))
    return pl.pallas_call(
        kernel,
        out_shape=outs,
        in_specs=[pl.BlockSpec(memory_space=VMEM) for _ in args],
        out_specs=[pl.BlockSpec(memory_space=VMEM) for _ in outs],
        scratch_shapes=list(scratch),
        cost_estimate=pl.CostEstimate(flops=flops, bytes_accessed=size, transcendentals=0),
        compiler_params=pltpu.CompilerParams(vmem_limit_bytes=40 << 20),
    )(*args)


def swap_cores(value):
    return lax.ppermute(value, "space", [(i, i ^ 1) for i in range(lax.axis_size("space"))])


def swap_chips(value):
    count = lax.axis_size("space")
    return lax.ppermute(value, "space", [(i, i + 1 if i % 2 else i - 1) for i in range(1, count - 1)])


def swaps(near, far):
    far = swap_chips(far)
    return swap_cores(near), far


def partner(value, mask):
    return lax.ppermute(value, "space", [(i, i ^ mask) for i in range(lax.axis_size("space"))])


def pairs_of_groups(block, first):
    count = lax.axis_size("depth")
    pairs = [(i, i + 1) for i in range(first, count - 1, 2)]
    return lax.ppermute(block, "depth", pairs + [(b, a) for a, b in pairs])


def body(c_points, adjoint_points, conv1_weight, conv2_weight, bias1):
    _, chans, height, breadth = c_points.shape
    layers = conv1_weight.shape[0]
    tiles = lax.axis_size("space")
    scale = 1.0 / math.sqrt(height * tiles * breadth)
    pix = height * breadth
    wide = 3 * chans
    S = jax.ShapeDtypeStruct
    tile32, tile16 = S((chans, pix), F32), S((chans, pix), BF16)
    rows16 = lambda rows: S((chans, rows * breadth), BF16)
    stack = lambda rows: S((wide, rows * breadth), BF16)
    row_flops = 2 * wide * wide * breadth

    s0, s0h = call(entry_kernel, [tile32, tile16], [c_points])
    near1 = swap_cores(s0h)
    q4, b3 = call(adjoint_kernel, [tile32, tile16], [adjoint_points])
    far1 = swap_chips(call(pack_kernel, [rows16(10)], [s0h, near1, b3])[0])
    mats = S((layers, 2, wide, wide), BF16)
    fw, bias = call(prepare_kernel, [mats, S((128, 8), F32)], [conv1_weight, conv2_weight, bias1])
    bw = call(turn_kernel, [mats], [conv1_weight, conv2_weight])[0]
    far1, fw, bias, bw = lax.optimization_barrier((far1, fw, bias, bw))
    near2 = swap_cores(call(pass_kernel, [rows16(6)], [far1, b3])[0])
    s3, x0, x1, x2, x3, a0, a1, a2, a3 = call(
        forward_kernel,
        [tile32, *[stack(6)] * 4, stack(6), stack(6), stack(10), stack(6)],
        [s0, near1, far1, near2, fw, bias],
        [VMEM((wide, 20 * breadth), BF16), VMEM((wide, 18 * breadth), BF16), VMEM((chans, 16 * breadth), F32)],
        flops=98 * row_flops,
    )
    f16 = call(last_kernel, [tile16], [s3, a3, fw], flops=6 * row_flops)[0]

    def single(pos, skip, base, adjoint, core, chip, hidden, final):
        outs = [tile32, tile16] if final is None else [tile16] * 2
        args = [adjoint, core, chip, hidden, bw]

        def kernel(*refs):
            given, refs = refs[: len(args)], refs[len(args) :]
            held = None if final is None else given[5]
            results, rest = refs[: len(outs)], refs[len(outs) :]
            single_kernel(pos, skip, base, *given[:5], held, results, *rest)

        if final is not None:
            args.append(final)
        return call(
            kernel,
            [*outs, tile16],
            args,
            [VMEM((wide, 8 * breadth), BF16), VMEM((wide, 6 * breadth), BF16)],
            flops=14 * row_flops,
        )

    def grads(skip, b, hidden, e, inputs):
        return call(
            functools.partial(grad_kernel, skip),
            [S((2, CHUNK, 128), F32)],
            [b, hidden, e, inputs],
            [VMEM((wide, 6 * breadth), BF16)] * 2,
            flops=12 * row_flops,
        )[0]

    q3, b2h, e3 = single(3, 0, (4, 8), q4, near2, far1, a3, None)
    near3, far3 = swaps(b2h, b2h)
    g3 = grads(0, b3, a3, e3, x3)
    q1, near4, far4, b0, b2, e2, b1, e1 = call(
        functools.partial(double_kernel, 2),
        [tile32, rows16(2), rows16(2), *[tile16] * 5],
        [q3, near3, far3, a2, a1, bw],
        [VMEM((wide, 12 * breadth), BF16), VMEM((wide, 10 * breadth), BF16), VMEM((chans, 8 * breadth), F32)],
        flops=36 * row_flops,
    )
    near4, far4, g3, f16 = lax.optimization_barrier((near4, far4, g3, f16))
    near4, far4 = swaps(near4, far4)
    g2 = grads(2, b2, a2, e2, x2)
    g1 = grads(0, b1, a1, e1, x1)
    square = S((wide, wide), F32)
    taps_scratch = [VMEM((wide, 6 * breadth), BF16)]
    two0 = call(two_kernel, [square], [b0, a0], taps_scratch, flops=6 * row_flops)[0]
    pair, far, e0 = single(0, 0, (0, 0), q1, near4, far4, a0, f16)
    g0 = call(one_kernel, [S((2, CHUNK, 128), F32)], [two0, e0, x0], taps_scratch, flops=6 * row_flops)[0]

    def chunks(n, kind):
        return S((n, CHUNK, 128), kind)

    send, keep = call(split_kernel, [chunks(4, BF16), chunks(4, F32)], [g0, g1, g2, g3])
    keep, *sends = call(spread_kernel, [chunks(1, F32)] + [chunks(1, BF16)] * 3, [keep, partner(send, 1)])
    parts = [partner(value, 2 * (k + 1)) for k, value in enumerate(sends)]
    far = pairs_of_groups(far, 1)
    pair = pairs_of_groups(pair, 0)
    mine = call(total_kernel, [chunks(1, BF16)], [keep, *parts])[0]
    parts = [partner(mine, 8 * (k + 1)) for k in range(3)]
    mine = call(total_kernel, [chunks(1, BF16)], [mine, *parts])[0]
    mine, pair, far = lax.optimization_barrier((mine, pair, far))
    parts = [partner(mine, 2 * (k + 1)) for k in range(3)]
    points, adjoints = call(
        points_kernel, [S(c_points.shape, F32), S(c_points.shape, F32)], [c_points, adjoint_points, pair, far]
    )
    mine = call(join_kernel, [chunks(4, BF16)], [mine, *parts])[0]
    mine, points, adjoints = lax.optimization_barrier((mine, points, adjoints))
    part = partner(mine, 1)
    one, two, vec = exit_calls(scale, mine, part, S(conv1_weight.shape, F32), S(bias1.shape, F32))
    return points, adjoints, one, two, vec


def solution(mesh):
    in_specs = (
        P("depth", None, "space", None),
        P("depth", None, "space", None),
        P("depth", None, None),
        P("depth", None, None),
        P("depth", None),
    )
    out_specs = in_specs[:2] + (P("depth", None, None), P("depth", None, None), P("depth", None))

    def run(*args):
        return tuple(body(*args))

    return jax.shard_map(run, mesh=mesh, in_specs=in_specs, out_specs=out_specs, check_vma=False)
```
